256 devices in a mesh: grp: 8 (over z), nb: 32 (over x, y, core).
Axes of the slice: x: 4, y: 4, z: 8, core: 2. Of those that a mesh axis runs over, the one named last changes fastest.
Arguments:
- hidden: bfloat16 [512, 64, 4096], P('nb')
- query_weight: bfloat16 [4096, 2048], P(None, 'grp')
- keys: bfloat16 [96, 128, 2048], P('nb', None, 'grp')
- values: bfloat16 [96, 128, 2048], P('nb', None, 'grp'), may hold values from -6 to 6
- neighbour_ids: int32 [512, 2], P('nb'), may hold values from 0 to 95, as said below
- neighbour_counts: int32 [512], P('nb'), may hold values from 1 to 2
- d_context: bfloat16 [512, 64, 2048], P('nb', None, 'grp'), may hold values from -6 to 6
Outputs:
- context: bfloat16 [512, 64, 2048], P('nb', None, 'grp')
- d_hidden: bfloat16 [512, 64, 4096], P('nb', None, 'grp')
- d_keys: bfloat16 [96, 128, 2048], P('nb', None, 'grp')
- d_values: bfloat16 [96, 128, 2048], P('nb', None, 'grp')
- d_weight: bfloat16 [4096, 2048], P('nb', 'grp')
The draws below stay inside these ranges and needn't reach their ends.
Inputs may be any that keep to these rules, and one draw needn't show every extreme that they name: `neighbour_ids`: block b belongs to index b // 3 of nb. The 32 references of the spans of one index of nb name the blocks of one index of nb at most 2 times; in every draw the blocks of some one index of nb are named exactly 2 times by the spans of every index of nb.
All inputs are finite; a program needn't handle non-finite values.
Results may differ from the reference program's by a relative error of at most 0.02.
The reference program's roundings to bfloat16 on the way count: a program that leaves them out, or rounds other values in their place, can miss the bound.
Values may be sent and summed in bfloat16 or wider, within the bound.
No kernel may reach another device: no remote copies, remote signals or barrier semaphores. Data moves between devices by JAX's collectives and lax.ppermute only.
A program may use at most 128 MiB of HBM per device.

```python
import math
import jax
import jax.numpy as jnp
from jax import lax

D = 4096
HEADS = 16
DH = 128
CT = 64
NT = 128
KN = 2
CH_DEV = 16
BLK_DEV = 3
SPANS = 512
NBLK = 96
CAP = 2
N_GRP = 8


def hidden_field(key):
    base = jax.random.fold_in(key, 101)
    return jax.random.normal(base, (SPANS, CT, D), jnp.float32)


def weight_field(key):
    base = jax.random.fold_in(key, 202)
    return jax.random.normal(base, (D, HEADS * DH), jnp.float32) / math.sqrt(D)


def neighbour_table(key):
    base = jax.random.fold_in(key, 303)
    key_owner, key_perm, key_local = jax.random.split(base, 3)
    device_total = SPANS // CH_DEV
    slot_total = device_total * CAP
    ref_total = CH_DEV * KN
    forced = jax.random.randint(key_owner, (), 0, device_total)
    slot_index = jnp.arange(slot_total, dtype=jnp.int32)

    def one_device(device_key):
        key_first, key_second = jax.random.split(device_key)
        ranking = jax.random.permutation(key_first, slot_total).astype(jnp.int32)
        ranking = jnp.where(slot_index // CAP == forced, -1 - slot_index % CAP, ranking)
        picked = jnp.argsort(ranking, stable=True)[:ref_total].astype(jnp.int32)
        shuffled = jax.random.permutation(key_second, picked)
        return (shuffled // CAP).astype(jnp.int32)
    owner_rows = jax.vmap(one_device)(jax.random.split(key_perm, device_total))
    local_rows = jax.random.randint(key_local, (device_total, ref_total), 0, BLK_DEV)
    return (owner_rows * BLK_DEV + local_rows).reshape(SPANS, KN).astype(jnp.int32)


def draw_hidden(key, part):
    return hidden_field(key).astype(jnp.bfloat16)


def draw_query_weight(key, part):
    return weight_field(key).astype(jnp.bfloat16)


def draw_neighbour_ids(key, part):
    return neighbour_table(key).astype(jnp.int32)


def draw_keys(key, part):
    base = jax.random.fold_in(key, 404)
    return jax.random.normal(base, (NBLK, NT, HEADS * DH), jnp.float32).astype(jnp.bfloat16)


def with_ends(result, key, low, high):
    shape = result.shape
    place = [jax.random.randint(jax.random.fold_in(key, axis), (), 0, shape[axis]) for axis in range(len(shape))]
    result = result.at[tuple(place)].set(low)
    longest = shape.index(max(shape))
    place[longest] = (place[longest] + 1) % shape[longest]
    return result.at[tuple(place)].set(high)


def shard_levels(key, extent, cuts, low, high):
    def one(axis_at, blocks):
        steps = jax.random.uniform(jax.random.fold_in(jax.random.fold_in(key, 6), axis_at), (blocks,), jnp.float32, low / len(cuts), high / len(cuts))
        return jnp.repeat(jnp.exp(steps), extent[axis_at] // blocks).reshape((-1,) + (1,) * (len(extent) - axis_at - 1))

    factor_of = one(*cuts[0])
    for cut in cuts[1:]:
        factor_of = factor_of * one(*cut)
    return factor_of


def noise(key, extent, deviation, most, pieces=(), kind=jnp.bfloat16):
    factor_of = shard_levels(key, extent, pieces, -0.22, 0.18) if pieces else 1.0
    entries = jax.random.normal(key, extent, jnp.float32) * deviation * factor_of
    return jnp.minimum(jnp.maximum(entries, -most), most).astype(kind)


def setup_inputs(seed: int = 0) -> dict:
    streams_of = jax.random.split(jax.random.key(seed), 8)
    hidden = draw_hidden(jax.random.fold_in(streams_of[7], 71), 0)
    query_weight = draw_query_weight(jax.random.fold_in(streams_of[7], 71), 0)
    keys = draw_keys(jax.random.fold_in(streams_of[7], 71), 0)
    values = noise(streams_of[3], (NBLK, NT, HEADS * DH), 1.0, 6.0, ((0, 32), (2, 8)))
    neighbour_ids = draw_neighbour_ids(jax.random.fold_in(streams_of[7], 71), 0)
    neighbour_counts = with_ends(jax.random.randint(streams_of[5], (SPANS,), 1, KN + 1), jax.random.fold_in(streams_of[5], 1), 1, KN).astype(jnp.int32)
    d_context = noise(streams_of[6], (SPANS, CT, HEADS * DH), 1.0, 6.0, ((0, 32), (2, 8)))
    return dict(hidden=hidden, query_weight=query_weight, keys=keys, values=values, neighbour_ids=neighbour_ids, neighbour_counts=neighbour_counts, d_context=d_context)


def reference(hidden, query_weight, keys, values, neighbour_ids, neighbour_counts, d_context):
    score_scale = 1.0 / math.sqrt(DH)
    head_cols = HEADS * DH
    group_cols = head_cols // N_GRP
    group_total = SPANS // CH_DEV
    weight_grouped = query_weight.astype(jnp.float32).reshape(D, N_GRP, group_cols)

    def one_group(carry, index):
        key_sums, value_sums, weight_sums = carry
        first_span = (index * CH_DEV).astype(jnp.int32)
        hidden_part = lax.dynamic_slice_in_dim(hidden, first_span, CH_DEV, 0)
        ids_part = lax.dynamic_slice_in_dim(neighbour_ids, first_span, CH_DEV, 0)
        counts_part = lax.dynamic_slice_in_dim(neighbour_counts, first_span, CH_DEV, 0)
        grad_part = lax.dynamic_slice_in_dim(d_context, first_span, CH_DEV, 0)
        hidden_rows = hidden_part.reshape(CH_DEV * CT, D)
        projected = jnp.dot(hidden_rows, query_weight, preferred_element_type=jnp.float32) * score_scale
        queries = projected.astype(jnp.bfloat16).reshape(CH_DEV, CT, HEADS, DH)
        flat_ids = ids_part.reshape(-1)
        key_rows = jnp.take(keys, flat_ids, axis=0).reshape(CH_DEV, KN * NT, HEADS, DH)
        value_rows = jnp.take(values, flat_ids, axis=0).reshape(CH_DEV, KN * NT, HEADS, DH)
        query_f = queries.astype(jnp.float32)
        key_f = key_rows.astype(jnp.float32)
        value_f = value_rows.astype(jnp.float32)
        scores = jnp.einsum('cthd,cuhd->chtu', query_f, key_f)
        position = lax.broadcasted_iota(jnp.int32, (1, 1, 1, KN * NT), 3)
        live_keys = position < (counts_part * NT)[:, None, None, None]
        scores = jnp.where(live_keys, scores, -jnp.inf)
        largest = lax.optimization_barrier(jnp.max(scores, axis=-1, keepdims=True))
        weights = jnp.exp(scores - largest)
        attention = weights / lax.optimization_barrier(jnp.sum(weights, axis=-1, keepdims=True))
        attention_low = attention.astype(jnp.bfloat16)
        attention_lf = attention_low.astype(jnp.float32)
        context = jnp.einsum('chtu,cuhd->cthd', attention_lf, value_f).astype(jnp.bfloat16)
        grad_heads = grad_part.reshape(CH_DEV, CT, HEADS, DH).astype(jnp.float32)
        grad_attention = jnp.einsum('cthd,cuhd->chtu', grad_heads, value_f)
        inner_sum = lax.optimization_barrier(jnp.sum(attention * grad_attention, axis=-1, keepdims=True))
        grad_scores = (attention * (grad_attention - inner_sum)).astype(jnp.bfloat16)
        grad_sf = grad_scores.astype(jnp.float32)
        grad_queries = (jnp.einsum('chtu,cuhd->cthd', grad_sf, key_f) * score_scale).astype(jnp.bfloat16)
        grad_keys = jnp.einsum('chtu,cthd->cuhd', grad_sf, query_f).astype(jnp.bfloat16)
        grad_values = jnp.einsum('chtu,cthd->cuhd', attention_lf, grad_heads).astype(jnp.bfloat16)
        key_sums = key_sums.at[flat_ids].add(grad_keys.reshape(CH_DEV * KN, NT, head_cols).astype(jnp.float32))
        value_sums = value_sums.at[flat_ids].add(grad_values.reshape(CH_DEV * KN, NT, head_cols).astype(jnp.float32))
        grad_rows = grad_queries.reshape(CH_DEV * CT, head_cols)
        weight_sums = weight_sums + lax.dot_general(hidden_rows, grad_rows, (((0,), (0,)), ((), ())), preferred_element_type=jnp.float32)
        grouped_rows = grad_rows.astype(jnp.float32).reshape(CH_DEV * CT, N_GRP, group_cols)
        partials = jnp.einsum('rgk,dgk->rgd', grouped_rows, weight_grouped).astype(jnp.bfloat16)
        partials = lax.optimization_barrier(partials)
        hidden_grad = lax.optimization_barrier(jnp.sum(partials.astype(jnp.float32), axis=1)).astype(jnp.bfloat16)
        outputs = (context.reshape(CH_DEV, CT, head_cols), hidden_grad.reshape(CH_DEV, CT, D))
        return ((key_sums, value_sums, weight_sums), outputs)
    start_carry = (jnp.zeros((NBLK, NT, head_cols), jnp.float32), jnp.zeros((NBLK, NT, head_cols), jnp.float32), jnp.zeros((D, head_cols), jnp.float32))
    final_carry, stacked = lax.scan(one_group, start_carry, jnp.arange(group_total, dtype=jnp.int32))
    key_sums, value_sums, weight_sums = final_carry
    context = stacked[0].reshape(SPANS, CT, head_cols)
    d_hidden = stacked[1].reshape(SPANS, CT, D)
    return (context, d_hidden, key_sums.astype(jnp.bfloat16), value_sums.astype(jnp.bfloat16), weight_sums.astype(jnp.bfloat16))
```

```python
import math

import jax
import jax.numpy as jnp
from jax import lax
from jax.experimental import pallas as pl
from jax.experimental.pallas import tpu as pltpu
from jax.sharding import PartitionSpec as P

DH = 128
SIDE = 4
CHIPS = SIDE * SIDE
F32 = jnp.float32
BF16 = jnp.bfloat16


def nb_perm(move):
    def flat(x, y, c):
        return (x * SIDE + y) * 2 + c

    return [
        (flat(x, y, c), flat(*move(x, y, c)))
        for x in range(SIDE)
        for y in range(SIDE)
        for c in range(2)
    ]


LINKS = (
    nb_perm(lambda x, y, c: (x ^ 1, y, c)),
    nb_perm(lambda x, y, c: (x, y ^ 1, c)),
    nb_perm(lambda x, y, c: (x ^ 3, y, c)),
    nb_perm(lambda x, y, c: (x, y ^ 3, c)),
)
SIBLING = nb_perm(lambda x, y, c: (x, y, c ^ 1))


def cube_bits(chip):
    x, y = chip // SIDE, chip % SIDE
    return ((x ^ (x >> 1)) & 1, (y ^ (y >> 1)) & 1, x >> 1, y >> 1)


def cube_place(mine, chip, stream):
    here, there = cube_bits(mine), cube_bits(chip)
    across = [a ^ b for a, b in zip(here, there)]
    return sum(across[(stream + k) % 4] << k for k in range(4))


def swap(value):
    return lax.ppermute(value, "nb", SIBLING)


def cube_gather(pieces):
    held = list(pieces)
    halves = None
    for k in range(4):
        came = [lax.ppermute(b, "nb", LINKS[(s + k) % 4]) for s, b in enumerate(held)]
        if k == 3:
            halves = [(b, r) for b, r in zip(held, came)]
        else:
            held = [jnp.concatenate([b, r], axis=0) for b, r in zip(held, came)]
    return halves


def summed(parts, start, stop):
    total = parts[0][start:stop].astype(F32)
    for p in parts[1:]:
        total = total + p[start:stop].astype(F32)
    return total


def cube_reduce(streams):
    low = [list(parts) for _, parts, _ in streams]
    high = [h for _, _, h in streams]
    size = high[0].shape[0]
    for k in (3, 2, 1, 0):
        came = [lax.ppermute(h, "nb", LINKS[(s[0] + k) % 4]) for s, h in zip(streams, high)]
        for parts, r in zip(low, came):
            parts.append(r)
        if k:
            size //= 2
            high = [summed(parts, size, 2 * size).astype(BF16) for parts in low]
    return [summed(parts, 0, size).astype(BF16) for parts in low]


def attention_body(
    slots, counts, q_own, q_sib, g_own, g_sib, k00, k01, k10, k11, v00, v01, v10, v11,
    ctx_own, ctx_sib, gq_own, gq_sib, dk00, dk01, dk10, dk11, dv00, dv01, dv10, dv11,
    k_all, v_all, dk_all, dv_all, in_sem, out_sem,
):
    scale = 1.0 / math.sqrt(DH)
    half = k00.shape[0]
    loads = []
    for n, ref in enumerate((k00, k01, k10, k11)):
        loads.append(pltpu.make_async_copy(ref, k_all.at[pl.ds(n * half, half)], in_sem.at[n]))
    for n, ref in enumerate((v00, v01, v10, v11)):
        loads.append(pltpu.make_async_copy(ref, v_all.at[pl.ds(n * half, half)], in_sem.at[4 + n]))
    for copy in loads:
        copy.start()
    blank = jnp.zeros(dk_all.shape[1:], BF16)

    def clear(n, carry):
        dk_all[n] = blank
        dv_all[n] = blank
        return carry

    lax.fori_loop(0, dk_all.shape[0], clear, 0, unroll=4)
    for copy in loads:
        copy.wait()

    def one_span(q_ref, g_ref, ctx_ref, gq_ref, i, span):
        q = q_ref[i]
        g = g_ref[i]
        ks = [slots[0, 2 * span], slots[0, 2 * span + 1]]
        vs = [slots[1, 2 * span], slots[1, 2 * span + 1]]
        k = jnp.concatenate([k_all[ks[0]], k_all[ks[1]]], axis=0)
        v = jnp.concatenate([v_all[vs[0]], v_all[vs[1]]], axis=0)
        rows = (((1,), (1,)), ((), ()))
        s = lax.dot_general(q, k, rows, preferred_element_type=F32)
        place = lax.broadcasted_iota(jnp.int32, s.shape, 1)
        s = jnp.where(place < counts[span] * k_all.shape[1], s, -jnp.inf)
        w = jnp.exp(s - jnp.max(s, axis=1, keepdims=True))
        a = w / jnp.sum(w, axis=1, keepdims=True)
        low = a.astype(BF16)
        ga = lax.dot_general(g, v, rows, preferred_element_type=F32)
        gs = (a * (ga - jnp.sum(a * ga, axis=1, keepdims=True))).astype(BF16)
        ctx_ref[i] = jnp.dot(low, v, preferred_element_type=F32).astype(BF16)
        gq_ref[i] = (jnp.dot(gs, k, preferred_element_type=F32) * scale).astype(BF16)
        cols = (((0,), (0,)), ((), ()))
        dk = lax.dot_general(gs, q, cols, preferred_element_type=F32).astype(BF16)
        dv = lax.dot_general(low, g, cols, preferred_element_type=F32).astype(BF16)
        n = k_all.shape[1]
        for j in range(2):
            part = dk[j * n : (j + 1) * n].astype(F32)
            dk_all[ks[j]] = (dk_all[ks[j]].astype(F32) + part).astype(BF16)
            part = dv[j * n : (j + 1) * n].astype(F32)
            dv_all[vs[j]] = (dv_all[vs[j]].astype(F32) + part).astype(BF16)

    spans = q_own.shape[0]

    def own_step(i, carry):
        one_span(q_own, g_own, ctx_own, gq_own, i, i)
        return carry

    def sib_step(i, carry):
        one_span(q_sib, g_sib, ctx_sib, gq_sib, i, i + spans)
        return carry

    lax.fori_loop(0, spans, own_step, 0, unroll=2)
    lax.fori_loop(0, spans, sib_step, 0, unroll=2)
    stores = []
    for n, ref in enumerate((dk00, dk01, dk10, dk11)):
        stores.append(pltpu.make_async_copy(dk_all.at[pl.ds(n * half, half)], ref, out_sem.at[n]))
    for n, ref in enumerate((dv00, dv01, dv10, dv11)):
        stores.append(pltpu.make_async_copy(dv_all.at[pl.ds(n * half, half)], ref, out_sem.at[4 + n]))
    for copy in stores:
        copy.start()
    for copy in stores:
        copy.wait()


def attention(slots, counts, q_own, q_sib, g_own, g_sib, k_halves, v_halves):
    spans, span_len, width = q_own.shape
    half, block_len, _ = k_halves[0].shape
    small = jax.ShapeDtypeStruct((spans, span_len, width), BF16)
    large = jax.ShapeDtypeStruct((half, block_len, width), BF16)
    whole = pltpu.VMEM((4 * half, block_len, width), BF16)
    in_smem = pl.BlockSpec(memory_space=pltpu.SMEM)
    in_vmem = pl.BlockSpec(memory_space=pltpu.VMEM)
    left = pl.BlockSpec(memory_space=pl.ANY)
    return pl.pallas_call(
        attention_body,
        out_shape=[small] * 4 + [large] * 8,
        in_specs=[in_smem] * 2 + [in_vmem] * 4 + [left] * 8,
        out_specs=[in_vmem] * 4 + [left] * 8,
        scratch_shapes=[whole] * 4 + [pltpu.SemaphoreType.DMA((8,)), pltpu.SemaphoreType.DMA((8,))],
        compiler_params=pltpu.CompilerParams(vmem_limit_bytes=32 * 2**20),
        name="attention",
    )(slots, counts, q_own, q_sib, g_own, g_sib, *k_halves, *v_halves)


def weight_body(places, gq_ref, hid_ref, own_a, own_b, sib, gq_t):
    step = pl.program_id(0)

    @pl.when(step == 0)
    def _():
        gq_t[...] = gq_ref[...].T

    term = jnp.dot(gq_t[...], hid_ref[...], preferred_element_type=F32).astype(BF16)
    part = own_a.shape[2]
    core = places[2, 0]
    for t in range(hid_ref.shape[1] // part):
        chip = step * (hid_ref.shape[1] // part // 2) + t // 2
        a, b = places[0, chip], places[1, chip]
        top = term[:DH, t * part : (t + 1) * part]
        bottom = term[DH:, t * part : (t + 1) * part]

        @pl.when(core == t % 2)
        def _():
            own_a[a] = top
            own_b[b] = bottom

        @pl.when(core != t % 2)
        def _():
            sib[0, a] = top
            sib[1, b] = bottom


def weight_terms(places, grad_rows, hidden_rows):
    rows, model_width = hidden_rows.shape
    part = model_width // (2 * CHIPS)
    wide = 4 * part
    stream = jax.ShapeDtypeStruct((CHIPS, DH, part), BF16)
    return pl.pallas_call(
        weight_body,
        out_shape=[stream, stream, jax.ShapeDtypeStruct((2, CHIPS, DH, part), BF16)],
        grid_spec=pltpu.PrefetchScalarGridSpec(
            num_scalar_prefetch=1,
            grid=(model_width // wide,),
            in_specs=[
                pl.BlockSpec(grad_rows.shape, lambda i, p: (0, 0)),
                pl.BlockSpec((rows, wide), lambda i, p: (0, i)),
            ],
            out_specs=[
                pl.BlockSpec((CHIPS, DH, part), lambda i, p: (0, 0, 0)),
                pl.BlockSpec((CHIPS, DH, part), lambda i, p: (0, 0, 0)),
                pl.BlockSpec((2, CHIPS, DH, part), lambda i, p: (0, 0, 0, 0)),
            ],
            scratch_shapes=[pltpu.VMEM(grad_rows.shape[::-1], BF16)],
        ),
        compiler_params=pltpu.CompilerParams(vmem_limit_bytes=32 * 2**20),
        name="weight_terms",
    )(places, grad_rows, hidden_rows)


def per_device(hidden, query_weight, keys, values, neighbour_ids, neighbour_counts, d_context):
    spans, span_len, model_width = hidden.shape
    blocks, block_len, head_cols = keys.shape
    groups = lax.axis_size("grp")
    scale = 1.0 / math.sqrt(DH)
    nb = lax.axis_index("nb")
    grp = lax.axis_index("grp")
    core = nb % 2
    chip = nb // 2
    rows = spans * span_len

    def head(array, which):
        return lax.dynamic_slice_in_dim(array, which * DH, DH, array.ndim - 1)

    with jax.named_scope("gather"):
        key_own, value_own = head(keys, core), head(values, core)
        key_sib = swap(head(keys, 1 - core))
        value_sib = swap(head(values, 1 - core))
        halves = cube_gather((key_own, key_sib, value_own, value_sib))
    with jax.named_scope("small"):
        table = jnp.concatenate([neighbour_ids.reshape(-1), neighbour_counts])
        table_sib = swap(table)
        grad_own = head(d_context, core)
        grad_sib = swap(head(d_context, 1 - core))
        refs = neighbour_ids.size
        ids = jnp.concatenate([table[:refs], table_sib[:refs]])
        counts = jnp.concatenate([table[refs:], table_sib[refs:]])
        owner, local = ids // blocks, ids % blocks
        near = owner % 2 == core

        def slot(near_stream, far_stream):
            place_near = cube_place(chip, owner // 2, near_stream) * blocks + local
            place_far = (CHIPS + cube_place(chip, owner // 2, far_stream)) * blocks + local
            return jnp.where(near, place_near, place_far)

        slots = jnp.stack([slot(0, 1), slot(2, 3)])
        every = jnp.arange(CHIPS, dtype=jnp.int32)
        places = jnp.stack(
            [cube_place(chip, every, 0), cube_place(chip, every, 1), jnp.broadcast_to(core, (CHIPS,))]
        )
    with jax.named_scope("queries"):
        hidden_rows = hidden.reshape(rows, model_width)
        projected = jnp.dot(hidden_rows, query_weight, preferred_element_type=F32) * scale
        queries = projected.astype(BF16).reshape(spans, span_len, head_cols)
        query_own = head(queries, core)
        query_sib = swap(head(queries, 1 - core))
    with jax.named_scope("weight_rows"):
        wide = model_width // groups
        weight_rows = []
        for k in range(groups):
            to = (grp + k) % groups
            mine = lax.dynamic_slice_in_dim(query_weight, to * wide, wide, 0)
            shift = [(i, (i + k) % groups) for i in range(groups)]
            weight_rows.append(lax.ppermute(mine, "grp", shift) if k else mine)
    with jax.named_scope("attend"):
        out = attention(
            slots, counts, query_own, query_sib, grad_own, grad_sib,
            (*halves[0], *halves[1]), (*halves[2], *halves[3]),
        )
        ctx_own, ctx_sib, gq_own, gq_sib = out[:4]
        grads = out[4:]

    def both_heads(own, other):
        pair = jnp.stack([own, other], axis=-2)
        pair = jnp.where(core == 0, pair, pair[..., ::-1, :])
        return pair.reshape(*own.shape[:-1], 2 * own.shape[-1])

    with jax.named_scope("grad_queries"):
        grad_rows = both_heads(gq_own, swap(gq_sib)).reshape(rows, head_cols)
    with jax.named_scope("return"):
        dk_own, dk_sib, dv_own, dv_sib = cube_reduce(
            [(s, [grads[2 * s]], grads[2 * s + 1]) for s in range(4)]
        )
        came = swap(jnp.concatenate([dk_sib, dv_sib], axis=0))
        d_keys = both_heads(dk_own, came[:blocks])
        d_values = both_heads(dv_own, came[blocks:])
    with jax.named_scope("context"):
        context = both_heads(ctx_own, swap(ctx_sib))
    with jax.named_scope("d_weight"):
        own_a, own_b, sib = weight_terms(places, grad_rows, hidden_rows)
        other = swap(sib)
        mid = CHIPS // 2
        tops = [(own_a[mid:].astype(F32) + other[0, mid:].astype(F32)).astype(BF16),
                (own_b[mid:].astype(F32) + other[1, mid:].astype(F32)).astype(BF16)]
        sum_a, sum_b = cube_reduce(
            [(0, [own_a, other[0]], tops[0]), (1, [own_b, other[1]], tops[1])]
        )
        d_weight = jnp.concatenate([sum_a[0], sum_b[0]], axis=0).T
    with jax.named_scope("d_hidden"):
        ahead = [(i, (i + 1) % groups) for i in range(groups)]
        behind = [(i, (i - 1) % groups) for i in range(groups)]

        def partial(piece, which):
            term = lax.dot_general(
                piece, weight_rows[which % groups], (((1,), (1,)), ((), ())), preferred_element_type=F32
            )
            return lax.reduce_precision(term, 8, 7)

        forward = backward = grad_rows
        total = partial(grad_rows, 0)
        reach = groups // 2
        for k in range(1, reach):
            forward = lax.ppermute(forward, "grp", ahead)
            backward = lax.ppermute(backward, "grp", behind)
            total = total + partial(forward, k)
            total = total + partial(backward, -k)
        last = jnp.concatenate(
            [
                lax.ppermute(forward[: rows // 2], "grp", ahead),
                lax.ppermute(backward[rows // 2 :], "grp", behind),
            ],
            axis=0,
        )
        total = total + partial(last, reach)
        d_hidden = total.astype(BF16).reshape(spans, span_len, wide)
    return context, d_hidden, d_keys, d_values, d_weight


def solution(mesh):
    placed = (
        P("nb", None, None),
        P(None, "grp"),
        P("nb", None, "grp"),
        P("nb", None, "grp"),
        P("nb", None),
        P("nb"),
        P("nb", None, "grp"),
    )
    return jax.shard_map(
        per_device,
        mesh=mesh,
        in_specs=placed,
        out_specs=(
            P("nb", None, "grp"),
            P("nb", None, "grp"),
            P("nb", None, "grp"),
            P("nb", None, "grp"),
            P("nb", "grp"),
        ),
        check_vma=False,
    )
```

```python
import math

import jax
import jax.numpy as jnp
from jax import lax
from jax.experimental import pallas as pl
from jax.experimental.pallas import tpu as pltpu
from jax.sharding import Mesh, PartitionSpec as P

DH = 128
SIDE = 4
CHIPS = SIDE * SIDE
NB = ("chip", "core")
F32 = jnp.float32
BF16 = jnp.bfloat16
VMEM_LIMIT = 40 * 2**20


def chip_pairs(move):
    pairs = []
    for x in range(SIDE):
        for y in range(SIDE):
            to_x, to_y = move(x, y)
            pairs.append((x * SIDE + y, to_x * SIDE + to_y))
    return pairs


LINKS = (
    chip_pairs(lambda x, y: (x ^ 1, y)),
    chip_pairs(lambda x, y: (x, y ^ 1)),
    chip_pairs(lambda x, y: (x ^ 3, y)),
    chip_pairs(lambda x, y: (x, y ^ 3)),
)


def cube_bits(chip):
    x, y = chip // SIDE, chip % SIDE
    return ((x ^ (x >> 1)) & 1, (y ^ (y >> 1)) & 1, x >> 1, y >> 1)


def cube_place(mine, chip, stream):
    here, there = cube_bits(mine), cube_bits(chip)
    across = [a ^ b for a, b in zip(here, there)]
    return sum(across[(stream + k) % 4] << k for k in range(4))


def swap(value):
    return lax.ppermute(value, "core", [(0, 1), (1, 0)])


def summed(parts, start, stop):
    total = 0.0
    for array, first in parts:
        total = total + array[first + start : first + stop].astype(F32)
    return total.astype(BF16)


def send(streams, k):
    came = [lax.ppermute(h, "chip", LINKS[(s + k) % 4]) for s, h in enumerate(streams)]
    return list(came)


def attention_body(
    slots, counts, q_own, q_sib, g_own, g_sib, k_in, v_in,
    ctx_own, gq_own, pair_sib, dk00, dk01, dk10, dk11, dv00, dv01, dv10, dv11,
    k_all, v_all, dk_all, dv_all, in_sem, out_sem,
):
    scale = 1.0 / math.sqrt(DH)
    block_len = k_all.shape[1]
    loads = [
        pltpu.make_async_copy(k_in, k_all, in_sem.at[0]),
        pltpu.make_async_copy(v_in, v_all, in_sem.at[1]),
    ]
    for copy in loads:
        copy.start()
    blank = jnp.zeros(dk_all.shape[1:], BF16)

    def clear(n, carry):
        dk_all[n] = blank
        dv_all[n] = blank
        return carry

    lax.fori_loop(0, dk_all.shape[0], clear, 0, unroll=4)
    for copy in loads:
        copy.wait()
    spans = q_own.shape[0]
    rows = (((1,), (1,)), ((), ()))
    cols = (((0,), (0,)), ((), ()))

    def step(i, carry):
        batch = [(q_own, g_own, i, i), (q_sib, g_sib, i, i + spans)]
        q = [qr[n] for qr, _, n, _ in batch]
        g = [gr[n] for _, gr, n, _ in batch]
        refs = [(2 * span, 2 * span + 1) for _, _, _, span in batch]
        k = [jnp.concatenate([k_all[slots[0, r]] for r in pair], axis=0) for pair in refs]
        v = [jnp.concatenate([v_all[slots[0, r]] for r in pair], axis=0) for pair in refs]
        s = [lax.dot_general(a, b, rows, preferred_element_type=F32) for a, b in zip(q, k)]
        ga = [lax.dot_general(a, b, rows, preferred_element_type=F32) for a, b in zip(g, v)]
        place = lax.broadcasted_iota(jnp.int32, s[0].shape, 1)
        s = [
            jnp.where(place < counts[span] * block_len, a, -jnp.inf)
            for a, (_, _, _, span) in zip(s, batch)
        ]
        w = [jnp.exp(a - jnp.max(a, axis=1, keepdims=True)) for a in s]
        att = [a / jnp.sum(a, axis=1, keepdims=True) for a in w]
        low = [a.astype(BF16) for a in att]
        gs = [
            (a * (b - jnp.sum(a * b, axis=1, keepdims=True))).astype(BF16)
            for a, b in zip(att, ga)
        ]
        ctx = [jnp.dot(a, b, preferred_element_type=F32).astype(BF16) for a, b in zip(low, v)]
        gq = [(jnp.dot(a, b, preferred_element_type=F32) * scale).astype(BF16) for a, b in zip(gs, k)]
        dk = [lax.dot_general(a, b, cols, preferred_element_type=F32).astype(BF16) for a, b in zip(gs, q)]
        dv = [lax.dot_general(a, b, cols, preferred_element_type=F32).astype(BF16) for a, b in zip(low, g)]
        ctx_own[i] = ctx[0]
        gq_own[i] = gq[0]
        pair_sib[0, i] = ctx[1]
        pair_sib[1, i] = gq[1]
        for n, pair in enumerate(refs):
            for j, r in enumerate(pair):
                at = slots[1, r]
                part = dk[n][j * block_len : (j + 1) * block_len].astype(F32)
                dk_all[at] = (dk_all[at].astype(F32) + part).astype(BF16)
                at = slots[2, r]
                part = dv[n][j * block_len : (j + 1) * block_len].astype(F32)
                dv_all[at] = (dv_all[at].astype(F32) + part).astype(BF16)
        return carry

    lax.fori_loop(0, spans, step, 0, unroll=2)
    half = dk00.shape[0]
    stores = []
    for n, ref in enumerate((dk00, dk01, dk10, dk11)):
        stores.append(pltpu.make_async_copy(dk_all.at[pl.ds(n * half, half)], ref, out_sem.at[n]))
    for n, ref in enumerate((dv00, dv01, dv10, dv11)):
        stores.append(pltpu.make_async_copy(dv_all.at[pl.ds(n * half, half)], ref, out_sem.at[4 + n]))
    for copy in stores:
        copy.start()
    for copy in stores:
        copy.wait()


def attention(slots, counts, q_own, q_sib, g_own, g_sib, k_in, v_in):
    spans, span_len, width = q_own.shape
    total, block_len, _ = k_in.shape
    small = jax.ShapeDtypeStruct((spans, span_len, width), BF16)
    pair = jax.ShapeDtypeStruct((2, spans, span_len, width), BF16)
    large = pltpu.HBM((total // 4, block_len, width), BF16)
    whole = pltpu.VMEM((total, block_len, width), BF16)
    in_smem = pl.BlockSpec(memory_space=pltpu.SMEM)
    in_vmem = pl.BlockSpec(memory_space=pltpu.VMEM)
    in_hbm = pl.BlockSpec(memory_space=pltpu.HBM)
    left = pl.BlockSpec(memory_space=pl.ANY)
    return pl.pallas_call(
        attention_body,
        out_shape=[small, small, pair] + [large] * 8,
        in_specs=[in_smem] * 2 + [in_vmem] * 4 + [left] * 2,
        out_specs=[in_vmem] * 3 + [in_hbm] * 8,
        scratch_shapes=[whole] * 4 + [pltpu.SemaphoreType.DMA((2,)), pltpu.SemaphoreType.DMA((8,))],
        compiler_params=pltpu.CompilerParams(vmem_limit_bytes=VMEM_LIMIT),
        name="attention",
    )(slots, counts, q_own, q_sib, g_own, g_sib, k_in, v_in)


def weight_body(places, gq_ref, hid_ref, own, sib, gq_t):
    step = pl.program_id(0)

    @pl.when(step == 0)
    def _():
        gq_t[...] = gq_ref[...].T

    term = jnp.dot(gq_t[...], hid_ref[...], preferred_element_type=F32).astype(BF16)
    streams, _, cut, part = own.shape
    core = places[streams, 0]
    per_step = hid_ref.shape[1] // part
    for t in range(per_step):
        chip = step * (per_step // 2) + t // 2
        pieces = [term[s * cut : (s + 1) * cut, t * part : (t + 1) * part] for s in range(streams)]

        @pl.when(core == t % 2)
        def _():
            for s in range(streams):
                own[s, places[s, chip]] = pieces[s]

        @pl.when(core != t % 2)
        def _():
            for s in range(streams):
                sib[s, places[s, chip]] = pieces[s]


def weight_terms(places, grad_rows, hidden_rows):
    rows, model_width = hidden_rows.shape
    head_cols = grad_rows.shape[1]
    part = model_width // (2 * CHIPS)
    wide = 4 * part
    shape = (4, CHIPS, head_cols // 4, part)
    return pl.pallas_call(
        weight_body,
        out_shape=[jax.ShapeDtypeStruct(shape, BF16)] * 2,
        grid_spec=pltpu.PrefetchScalarGridSpec(
            num_scalar_prefetch=1,
            grid=(model_width // wide,),
            in_specs=[
                pl.BlockSpec(grad_rows.shape, lambda i, p: (0, 0)),
                pl.BlockSpec((rows, wide), lambda i, p: (0, i)),
            ],
            out_specs=[pl.BlockSpec(shape, lambda i, p: (0, 0, 0, 0))] * 2,
            scratch_shapes=[pltpu.VMEM(grad_rows.shape[::-1], BF16)],
        ),
        compiler_params=pltpu.CompilerParams(vmem_limit_bytes=VMEM_LIMIT),
        name="weight_terms",
    )(places, grad_rows, hidden_rows)


def hidden_body(gq_ref, w_ref, out):
    total = None
    for g in range(gq_ref.shape[0]):
        term = lax.dot_general(
            gq_ref[g], w_ref[g], (((1,), (1,)), ((), ())), preferred_element_type=F32
        )
        term = term.astype(BF16).astype(F32)
        total = term if total is None else total + term
    out[...] = total.astype(BF16)


def hidden_grads(every_grad, weight_rows):
    groups, rows, head_cols = every_grad.shape
    wide = weight_rows.shape[1]
    chunk = rows // 4
    return pl.pallas_call(
        hidden_body,
        out_shape=jax.ShapeDtypeStruct((rows, wide), BF16),
        grid=(rows // chunk,),
        in_specs=[
            pl.BlockSpec((groups, chunk, head_cols), lambda i: (0, i, 0)),
            pl.BlockSpec(weight_rows.shape, lambda i: (0, 0, 0)),
        ],
        out_specs=pl.BlockSpec((chunk, wide), lambda i: (i, 0)),
        compiler_params=pltpu.CompilerParams(vmem_limit_bytes=VMEM_LIMIT),
        name="hidden_grads",
    )(every_grad, weight_rows)


def per_device(hidden, query_weight, keys, values, neighbour_ids, neighbour_counts, d_context):
    spans, span_len, model_width = hidden.shape
    blocks, block_len, head_cols = keys.shape
    groups = lax.axis_size("grp")
    scale = 1.0 / math.sqrt(DH)
    chip = lax.axis_index("chip")
    core = lax.axis_index("core")
    rows = spans * span_len
    refs = neighbour_ids.size

    def both(array):
        first, second = array[..., :DH], array[..., DH:]
        return jnp.where(core == 0, first, second), jnp.where(core == 0, second, first)

    def joined(own, other):
        return jnp.where(
            core == 0,
            jnp.concatenate([own, other], axis=-1),
            jnp.concatenate([other, own], axis=-1),
        )

    with jax.named_scope("gather"):
        own, other = both(jnp.stack([keys, values]))
        came = swap(other)
        every_key = lax.all_gather(jnp.concatenate([own[0], came[0]]), "chip", axis=0, tiled=True)
        every_value = lax.all_gather(jnp.concatenate([own[1], came[1]]), "chip", axis=0, tiled=True)
    with jax.named_scope("weight_rows"):
        wide = model_width // groups
        weight_rows = lax.all_to_all(query_weight, "grp", split_axis=0, concat_axis=0, tiled=True)
        weight_rows = weight_rows.reshape(groups, wide, head_cols)
    with jax.named_scope("queries"):
        hidden_rows = hidden.reshape(rows, model_width)
        projected = jnp.dot(hidden_rows, query_weight, preferred_element_type=F32) * scale
        queries = projected.astype(BF16).reshape(spans, span_len, head_cols)
        query_own, query_other = both(queries)
        grad_own, grad_other = both(d_context)
        came = swap(jnp.stack([query_other, grad_other]))
        query_sib, grad_sib = came[0], came[1]
    with jax.named_scope("slots"):
        table = jnp.concatenate([neighbour_ids.reshape(-1), neighbour_counts])
        table_sib = swap(table)
        ids = jnp.concatenate([table[:refs], table_sib[:refs]])
        counts = jnp.concatenate([table[refs:], table_sib[refs:]])
        owner, local = ids // blocks, ids % blocks
        far = jnp.where(owner % 2 == core, 0, 1)
        host = owner // 2

        def slot(near_stream, far_stream):
            near_place = cube_place(chip, host, near_stream)
            far_place = CHIPS + cube_place(chip, host, far_stream)
            return jnp.where(far == 0, near_place, far_place) * blocks + local

        slots = jnp.stack([(host * 2 + far) * blocks + local, slot(0, 1), slot(2, 3)])
        every = jnp.arange(CHIPS, dtype=jnp.int32)
        places = jnp.stack(
            [cube_place(chip, every, s) for s in range(4)] + [jnp.broadcast_to(core, (CHIPS,))]
        )
    with jax.named_scope("attend"):
        out = attention(
            slots, counts, query_own, query_sib, grad_own, grad_sib, every_key, every_value
        )
        ctx_own, gq_own, pair_sib = out[:3]
        low = [g.reshape(-1, DH) for g in out[3::2]]
        high = [g.reshape(-1, DH) for g in out[4::2]]
    with jax.named_scope("grad_queries"):
        pair = swap(pair_sib)
        context = joined(ctx_own, pair[0])
        grad_rows = joined(gq_own, pair[1]).reshape(rows, head_cols)
        every_grad = lax.all_gather(grad_rows, "grp", axis=0, tiled=False)
    with jax.named_scope("return"):
        came = send(high, 3)
        terms, terms_sib = weight_terms(places, grad_rows, hidden_rows)
        cut = terms.shape[2]
        terms = terms.reshape(4, -1, DH)
        others = swap(terms_sib).reshape(4, -1, DH)
        span = terms.shape[1] // 2
        kv = [[(a, 0), (b, 0)] for a, b in zip(low, came)]
        dw = [[(terms[s], 0), (others[s], 0)] for s in range(4)]
        came_w = send([summed(p, span, 2 * span) for p in dw], 3)
        for s in range(4):
            dw[s].append((came_w[s], 0))
        size = low[0].shape[0]
        for k in (2, 1, 0):
            size //= 2
            span //= 2
            packed = [
                jnp.concatenate([summed(a, size, 2 * size), summed(b, span, 2 * span)])
                for a, b in zip(kv, dw)
            ]
            packed = lax.optimization_barrier(packed)
            came = send(packed, k)
            came = lax.optimization_barrier(came)
            for s in range(4):
                kv[s].append((came[s], 0))
                dw[s].append((came[s], size))
        kv = [summed(p, 0, size) for p in kv]
        dw = [summed(p, 0, span) for p in dw]
        other = swap(jnp.concatenate([kv[1], kv[3]]))
        d_keys = joined(kv[0], other[:size]).reshape(blocks, block_len, head_cols)
        d_values = joined(kv[2], other[size:]).reshape(blocks, block_len, head_cols)
        d_weight = jnp.concatenate(dw).T
    with jax.named_scope("d_hidden"):
        d_hidden = hidden_grads(every_grad, weight_rows).reshape(spans, span_len, wide)
    return context, d_hidden, d_keys, d_values, d_weight


def solution(mesh):
    fine = Mesh(mesh.devices.reshape(mesh.devices.shape[0], CHIPS, 2), ("grp", "chip", "core"))
    placed = (
        P(NB, None, None),
        P(None, "grp"),
        P(NB, None, "grp"),
        P(NB, None, "grp"),
        P(NB, None),
        P(NB),
        P(NB, None, "grp"),
    )
    return jax.shard_map(
        per_device,
        mesh=fine,
        in_specs=placed,
        out_specs=(
            P(NB, None, "grp"),
            P(NB, None, "grp"),
            P(NB, None, "grp"),
            P(NB, None, "grp"),
            P(NB, "grp"),
        ),
        check_vma=False,
    )
```

```python
import math

import jax
import jax.numpy as jnp
from jax import lax
from jax.experimental import pallas as pl
from jax.experimental.pallas import tpu as pltpu
from jax.sharding import Mesh, PartitionSpec as P

DH = 128
SIDE = 4
CHIPS = SIDE * SIDE
NB = ("chip", "core")
F32 = jnp.float32
BF16 = jnp.bfloat16
MIB = 2**20


def chip_pairs(move):
    pairs = []
    for x in range(SIDE):
        for y in range(SIDE):
            to_x, to_y = move(x, y)
            pairs.append((x * SIDE + y, to_x * SIDE + to_y))
    return pairs


LINKS = (
    chip_pairs(lambda x, y: (x ^ 1, y)),
    chip_pairs(lambda x, y: (x, y ^ 1)),
    chip_pairs(lambda x, y: (x ^ 3, y)),
    chip_pairs(lambda x, y: (x, y ^ 3)),
)


def cube_bits(chip):
    x, y = chip // SIDE, chip % SIDE
    return ((x ^ (x >> 1)) & 1, (y ^ (y >> 1)) & 1, x >> 1, y >> 1)


ORDERS = ((0, 1, 3, 2), (0, 1, 2, 3), (2, 3, 1, 0), (2, 3, 0, 1))


GATHER_ORDERS = ((0, 1, 2, 3), (1, 2, 3, 0), (2, 3, 0, 1), (3, 0, 1, 2))


def cube_place(mine, chip, order):
    here, there = cube_bits(mine), cube_bits(chip)
    across = [a ^ b for a, b in zip(here, there)]
    return sum(across[d] << k for k, d in enumerate(order))


def square_pairs(pair, bits):
    moves = [dict(LINKS[d]) for k, d in enumerate(ORDERS[2 * pair][:2]) if bits >> k & 1]
    pairs = []
    for start in range(CHIPS):
        to = start
        for move in moves:
            to = move[to]
        pairs.append((start, to))
    return pairs


def swap(value):
    return lax.ppermute(value, "core", [(0, 1), (1, 0)])


def send(streams, k):
    return [lax.ppermute(h, "chip", LINKS[ORDERS[s][k]]) for s, h in enumerate(streams)]


def in_hbm(array):
    return pltpu.with_memory_space_constraint(array, pltpu.HBM)


def add_up(block, *refs):
    total = refs[0][block].astype(F32)
    for ref in refs[1:]:
        total = total + ref[block].astype(F32)
    return total


def half_body(kept, came, out, held, sem, offset):
    size = held.shape[1]
    loads = [pltpu.make_async_copy(kept[s], held.at[s], sem.at[s]) for s in range(4)]
    for copy in loads:
        copy.start()
    for s in range(4):
        loads[s].wait()

        def step(i, carry):
            total = held[s, i].astype(F32) + came[s][offset + i].astype(F32)
            out[s][i] = total.astype(BF16)
            return carry

        lax.fori_loop(0, size, step, 0, unroll=4)


def in_vmem(body, name, out_shape, *operands):
    vmem = pl.BlockSpec(memory_space=pltpu.VMEM)
    return pl.pallas_call(
        body,
        out_shape=out_shape,
        in_specs=[vmem] * len(operands),
        out_specs=[vmem] * len(out_shape),
        compiler_params=pltpu.CompilerParams(vmem_limit_bytes=6 * MIB),
        name=name,
    )(*operands)


def combine_half(name, kept, came, offset):
    def body(*refs):
        half_body(refs[:4], refs[4:8], refs[8:12], *refs[12:], offset)

    vmem = pl.BlockSpec(memory_space=pltpu.VMEM)
    return pl.pallas_call(
        body,
        out_shape=[jax.ShapeDtypeStruct(kept[0].shape, BF16)] * 4,
        in_specs=[pl.BlockSpec(memory_space=pl.ANY)] * 4 + [vmem] * 4,
        out_specs=[vmem] * 4,
        scratch_shapes=[pltpu.VMEM((4, *kept[0].shape), BF16), pltpu.SemaphoreType.DMA((4,))],
        compiler_params=pltpu.CompilerParams(vmem_limit_bytes=6 * MIB),
        name=name,
    )(*[in_hbm(k) for k in kept], *came)


def square_body(*refs):
    cut = refs[0].shape[0] // 4
    mine = refs[14]

    def step(i, carry):
        for s in range(4):
            for m in range(3):
                total = add_up((m + 1) * cut + i, refs[s], refs[4 + s])
                refs[8 + s // 2 * 3 + m][s % 2, i] = total.astype(BF16)
            mine[s, i] = add_up(i, refs[s], refs[4 + s])
        return carry

    lax.fori_loop(0, cut, step, 0)


def combine_square(kept, came):
    size, block_len, width = kept[0].shape
    shape = jax.ShapeDtypeStruct((2, size // 4, block_len, width), BF16)
    mine = jax.ShapeDtypeStruct((4, size // 4, block_len, width), F32)
    return in_vmem(square_body, "combine_square", [shape] * 6 + [mine], *kept, *came)


def last_body(mine_in, *refs):
    came, (out_own, out_sib), (mine, held, sem) = refs[:6], refs[6:8], refs[8:]
    loads = [pltpu.make_async_copy(mine_in, mine, sem.at[6])]
    for n in range(6):
        loads.append(pltpu.make_async_copy(came[n], held.at[n], sem.at[n]))
    for copy in loads:
        copy.start()
    for copy in loads:
        copy.wait()

    def step(i, carry):
        for s in range(4):
            pair = s // 2
            total = mine[s, i]
            for n in range(3 * pair, 3 * pair + 3):
                total = total + held[n, s % 2, i].astype(F32)
            (out_sib if s % 2 else out_own)[pair, i] = total.astype(BF16)
        return carry

    lax.fori_loop(0, mine.shape[1], step, 0)


def combine_last(mine, square):
    part = (2, *mine.shape[1:])
    left = pl.BlockSpec(memory_space=pl.ANY)
    vmem = pl.BlockSpec(memory_space=pltpu.VMEM)
    return pl.pallas_call(
        last_body,
        out_shape=[jax.ShapeDtypeStruct(part, BF16)] * 2,
        in_specs=[left] * 7,
        out_specs=[vmem] * 2,
        scratch_shapes=[
            pltpu.VMEM(mine.shape, F32),
            pltpu.VMEM((6, *part), BF16),
            pltpu.SemaphoreType.DMA((7,)),
        ],
        compiler_params=pltpu.CompilerParams(vmem_limit_bytes=6 * MIB),
        name="combine_last",
    )(mine, *[in_hbm(a) for a in square])


def join_body(*refs):
    size = refs[0].shape[0]

    def step(i, carry):
        for s in range(4):
            refs[8 + s][i] = refs[s][i]
            refs[8 + s][size + i] = refs[4 + s][i]
        return carry

    lax.fori_loop(0, size, step, 0, unroll=2)


def join_halves(held, came):
    shape = jax.ShapeDtypeStruct((2 * held[0].shape[0], *held[0].shape[1:]), BF16)
    return in_vmem(join_body, "join_halves", [shape] * 4, *held, *came)


def project_body(core, hid_ref, w_ref, own, other):
    scale = 1.0 / math.sqrt(DH)
    both = jnp.dot(hid_ref[...], w_ref[...], preferred_element_type=F32) * scale
    first, second = both[:, :DH].astype(BF16), both[:, DH:].astype(BF16)

    @pl.when(core[0] == 0)
    def _():
        own[...] = first
        other[...] = second

    @pl.when(core[0] != 0)
    def _():
        own[...] = second
        other[...] = first


def project(core, hidden_rows, query_weight):
    rows, model_width = hidden_rows.shape
    chunk = rows // 8
    out_spec = pl.BlockSpec((chunk, DH), lambda i, p: (i, 0))
    return pl.pallas_call(
        project_body,
        out_shape=[jax.ShapeDtypeStruct((rows, DH), BF16)] * 2,
        grid_spec=pltpu.PrefetchScalarGridSpec(
            num_scalar_prefetch=1,
            grid=(rows // chunk,),
            in_specs=[
                pl.BlockSpec((chunk, model_width), lambda i, p: (i, 0)),
                pl.BlockSpec(query_weight.shape, lambda i, p: (0, 0)),
            ],
            out_specs=[out_spec] * 2,
        ),
        compiler_params=pltpu.CompilerParams(vmem_limit_bytes=12 * MIB),
        name="project",
    )(core, in_hbm(hidden_rows), query_weight)


def weight_sum_body(terms, out):
    total = terms[0].astype(F32)
    for n in range(1, terms.shape[0]):
        total = total + terms[n].astype(F32)
    out[...] = total.T.astype(BF16)


def weight_sum(terms):
    _, head_cols, part = terms.shape
    shape = jax.ShapeDtypeStruct((part, head_cols), BF16)
    return in_vmem(weight_sum_body, "weight_sum", [shape], terms)[0]


def attention_body(
    slots, counts, q_own, q_sib, g_own, g_sib, *refs
):
    kv_in, (ctx_own, gq_own, pair_sib), outs = refs[:8], refs[8:11], refs[11:23]
    kv_all, dk_all, dv_all, in_sem, out_sem = refs[23:]
    scale = 1.0 / math.sqrt(DH)
    block_len = kv_all.shape[1]
    half = dk_all.shape[0] // 4
    loads = []
    for n, ref in enumerate(kv_in):
        part = kv_all.at[pl.ds(n * half, half)]
        loads.append(pltpu.make_async_copy(ref, part, in_sem.at[n]))
    for copy in loads:
        copy.start()
    blank = jnp.zeros(dk_all.shape[1:], BF16)

    def clear(n, carry):
        dk_all[n] = blank
        dv_all[n] = blank
        return carry

    lax.fori_loop(0, dk_all.shape[0], clear, 0, unroll=4)
    for copy in loads:
        copy.wait()
    spans = q_own.shape[0]
    rows = (((1,), (1,)), ((), ()))
    cols = (((0,), (0,)), ((), ()))

    def step(i, carry):
        batch = [(q_own, g_own, i, i), (q_sib, g_sib, i, i + spans)]
        q = [qr[n] for qr, _, n, _ in batch]
        g = [gr[n] for _, gr, n, _ in batch]
        refs = [(2 * span, 2 * span + 1) for _, _, _, span in batch]
        k = [jnp.concatenate([kv_all[slots[0, r]] for r in pair], axis=0) for pair in refs]
        v = [jnp.concatenate([kv_all[slots[1, r]] for r in pair], axis=0) for pair in refs]
        s = [lax.dot_general(a, b, rows, preferred_element_type=F32) for a, b in zip(q, k)]
        ga = [lax.dot_general(a, b, rows, preferred_element_type=F32) for a, b in zip(g, v)]
        place = lax.broadcasted_iota(jnp.int32, s[0].shape, 1)
        s = [
            jnp.where(place < counts[span] * block_len, a, -jnp.inf)
            for a, (_, _, _, span) in zip(s, batch)
        ]
        w = [jnp.exp(a - jnp.max(a, axis=1, keepdims=True)) for a in s]
        att = [a / jnp.sum(a, axis=1, keepdims=True) for a in w]
        low = [a.astype(BF16) for a in att]
        gs = [
            (a * (b - jnp.sum(a * b, axis=1, keepdims=True))).astype(BF16)
            for a, b in zip(att, ga)
        ]
        ctx = [jnp.dot(a, b, preferred_element_type=F32).astype(BF16) for a, b in zip(low, v)]
        gq = [(jnp.dot(a, b, preferred_element_type=F32) * scale).astype(BF16) for a, b in zip(gs, k)]
        dk = [lax.dot_general(a, b, cols, preferred_element_type=F32).astype(BF16) for a, b in zip(gs, q)]
        dv = [lax.dot_general(a, b, cols, preferred_element_type=F32).astype(BF16) for a, b in zip(low, g)]
        ctx_own[i] = ctx[0]
        gq_own[i] = gq[0]
        pair_sib[0, i] = ctx[1]
        pair_sib[1, i] = gq[1]
        for n, pair in enumerate(refs):
            for j, r in enumerate(pair):
                at = slots[2, r]
                part = dk[n][j * block_len : (j + 1) * block_len].astype(F32)
                dk_all[at] = (dk_all[at].astype(F32) + part).astype(BF16)
                at = slots[3, r]
                part = dv[n][j * block_len : (j + 1) * block_len].astype(F32)
                dv_all[at] = (dv_all[at].astype(F32) + part).astype(BF16)
        return carry

    lax.fori_loop(0, spans, step, 0, unroll=2)
    stores = []
    for s in range(4):
        whole = dk_all if s < 2 else dv_all
        at = s % 2 * 2 * half
        for ref in outs[3 * s : 3 * s + 3]:
            size = ref.shape[0]
            stores.append(
                pltpu.make_async_copy(whole.at[pl.ds(at, size)], ref, out_sem.at[len(stores)])
            )
            at += size
    for copy in stores:
        copy.start()
    for copy in stores:
        copy.wait()


def attention(slots, counts, q_own, q_sib, g_own, g_sib, gathered):
    spans, span_len, width = q_own.shape
    half, block_len, _ = gathered[0].shape
    small = jax.ShapeDtypeStruct((spans, span_len, width), BF16)
    pair = jax.ShapeDtypeStruct((2, spans, span_len, width), BF16)
    pieces = [half // 2, half // 2, half] * 4
    large = [pltpu.HBM((n, block_len, width), BF16) for n in pieces]
    grads = pltpu.VMEM((4 * half, block_len, width), BF16)
    smem = pl.BlockSpec(memory_space=pltpu.SMEM)
    vmem = pl.BlockSpec(memory_space=pltpu.VMEM)
    hbm = pl.BlockSpec(memory_space=pltpu.HBM)
    left = pl.BlockSpec(memory_space=pl.ANY)
    return pl.pallas_call(
        attention_body,
        out_shape=[small, small, pair] + large,
        in_specs=[smem] * 2 + [vmem] * 4 + [left] * 8,
        out_specs=[vmem] * 3 + [hbm] * 12,
        scratch_shapes=[
            pltpu.VMEM((8 * half, block_len, width), BF16),
            grads,
            grads,
            pltpu.SemaphoreType.DMA((8,)),
            pltpu.SemaphoreType.DMA((12,)),
        ],
        compiler_params=pltpu.CompilerParams(vmem_limit_bytes=20 * MIB),
        name="attention",
    )(slots, counts, q_own, q_sib, g_own, g_sib, *gathered)


def weight_body(core, gq_ref, hid_ref, own, sib, gq_t):
    step = pl.program_id(0)

    @pl.when(step == 0)
    def _():
        gq_t[...] = gq_ref[...].T

    term = jnp.dot(gq_t[...], hid_ref[...], preferred_element_type=F32).astype(BF16)
    chips, _, part = own.shape
    for n in range(chips):
        even = term[:, 2 * n * part : (2 * n + 1) * part]
        odd = term[:, (2 * n + 1) * part : (2 * n + 2) * part]

        @pl.when(core[0] == 0)
        def _():
            own[n] = even
            sib[n] = odd

        @pl.when(core[0] != 0)
        def _():
            own[n] = odd
            sib[n] = even


def weight_terms(core, grad_rows, hidden_rows):
    rows, model_width = hidden_rows.shape
    head_cols = grad_rows.shape[1]
    part = model_width // (2 * CHIPS)
    chips = 2
    wide = 2 * chips * part
    out_spec = pl.BlockSpec((chips, head_cols, part), lambda i, p: (i, 0, 0))
    return pl.pallas_call(
        weight_body,
        out_shape=[jax.ShapeDtypeStruct((CHIPS, head_cols, part), BF16)] * 2,
        grid_spec=pltpu.PrefetchScalarGridSpec(
            num_scalar_prefetch=1,
            grid=(CHIPS // chips,),
            in_specs=[
                pl.BlockSpec(grad_rows.shape, lambda i, p: (0, 0)),
                pl.BlockSpec((rows, wide), lambda i, p: (0, i)),
            ],
            out_specs=[out_spec] * 2,
            scratch_shapes=[pltpu.VMEM(grad_rows.shape[::-1], BF16)],
        ),
        compiler_params=pltpu.CompilerParams(vmem_limit_bytes=12 * MIB),
        name="weight_terms",
    )(core, grad_rows, in_hbm(hidden_rows))


def hidden_body(core, gq_ref, mine, other, out):
    wide = mine.shape[1]
    for n, w_ref in enumerate((mine, other)):
        total = None
        for g in range(gq_ref.shape[0]):
            term = lax.dot_general(
                gq_ref[g], w_ref[g], (((1,), (1,)), ((), ())), preferred_element_type=F32
            )
            term = term.astype(BF16).astype(F32)
            total = term if total is None else total + term
        at = pl.multiple_of((core[0] if n == 0 else 1 - core[0]) * wide, wide)
        out[:, pl.ds(at, wide)] = total.astype(BF16)


def hidden_grads(core, every_grad, mine, other):
    groups, rows, head_cols = every_grad.shape
    wide = 2 * mine.shape[1]
    chunk = rows // 4
    return pl.pallas_call(
        hidden_body,
        out_shape=jax.ShapeDtypeStruct((rows, wide), BF16),
        grid_spec=pltpu.PrefetchScalarGridSpec(
            num_scalar_prefetch=1,
            grid=(rows // chunk,),
            in_specs=[
                pl.BlockSpec((groups, chunk, head_cols), lambda i, p: (0, i, 0)),
                pl.BlockSpec(mine.shape, lambda i, p: (0, 0, 0)),
                pl.BlockSpec(mine.shape, lambda i, p: (0, 0, 0)),
            ],
            out_specs=pl.BlockSpec((chunk, wide), lambda i, p: (i, 0)),
        ),
        compiler_params=pltpu.CompilerParams(vmem_limit_bytes=16 * MIB),
        name="hidden_grads",
    )(core, in_hbm(every_grad), mine, other)


def per_device(hidden, query_weight, keys, values, neighbour_ids, neighbour_counts, d_context):
    spans, span_len, model_width = hidden.shape
    blocks, block_len, head_cols = keys.shape
    groups = lax.axis_size("grp")
    chip = lax.axis_index("chip")
    core = lax.axis_index("core")
    core_at = core.reshape(1)
    rows = spans * span_len
    refs = neighbour_ids.size

    def both(array):
        first, second = array[..., :DH], array[..., DH:]
        return jnp.where(core == 0, first, second), jnp.where(core == 0, second, first)

    def joined(own, other):
        return jnp.where(
            core == 0,
            jnp.concatenate([own, other], axis=-1),
            jnp.concatenate([other, own], axis=-1),
        )

    with jax.named_scope("gather"):
        own, other = both(jnp.stack([keys, values]))
        came = swap(other)
        held = list(lax.optimization_barrier([own[0], came[0], own[1], came[1]]))
        def across(pieces, k):
            return [lax.ppermute(p, "chip", LINKS[GATHER_ORDERS[s][k]]) for s, p in enumerate(pieces)]

        for k in range(2):
            came = across(held, k)
            held = [jnp.concatenate([a, b]) for a, b in zip(held, came)]
        held = join_halves(held, across(held, 2))
        last = across(held, 3)
    with jax.named_scope("queries"):
        hidden_rows = hidden.reshape(rows, model_width)
        query_own, query_other = project(core_at, hidden_rows, query_weight)
        query_own, query_other, leaving = lax.optimization_barrier(
            (query_own, query_other, query_weight)
        )
        last, query_own, query_other = lax.optimization_barrier((last, query_own, query_other))
        gathered = [part for parts in zip(held, last) for part in parts]
        query_own = query_own.reshape(spans, span_len, DH)
        query_sib = swap(query_other.reshape(spans, span_len, DH))
    with jax.named_scope("weight_rows"):
        wide = model_width // groups
        asked = leaving.reshape(groups, 2, wide // 2, head_cols)
        asked = jnp.where(core == 0, asked[:, 0], asked[:, 1])
        weight_own = lax.all_to_all(asked, "grp", split_axis=0, concat_axis=0, tiled=True)
    with jax.named_scope("more"):
        grad_own, grad_other = both(d_context)
        grad_sib = swap(grad_other)
    with jax.named_scope("slots"):
        table = jnp.concatenate([neighbour_ids.reshape(-1), neighbour_counts])
        table_sib = swap(table)
        ids = jnp.concatenate([table[:refs], table_sib[:refs]])
        counts = jnp.concatenate([table[refs:], table_sib[refs:]])
        owner, local = ids // blocks, ids % blocks
        far = jnp.where(owner % 2 == core, 0, 1)
        host = owner // 2

        def slot(orders, first):
            near_place = cube_place(chip, host, orders[0])
            far_place = CHIPS + cube_place(chip, host, orders[1])
            return (first + jnp.where(far == 0, near_place, far_place)) * blocks + local

        slots = jnp.stack(
            [
                slot(GATHER_ORDERS[:2], 0),
                slot(GATHER_ORDERS[2:], 2 * CHIPS),
                slot(ORDERS[:2], 0),
                slot(ORDERS[2:], 0),
            ]
        )
    with jax.named_scope("attend"):
        out = attention(slots, counts, query_own, query_sib, grad_own, grad_sib, gathered)
        ctx_own, gq_own, pair_sib = out[:3]
        low, mid, high = out[3::3], out[4::3], out[5::3]
    with jax.named_scope("grad_queries"):
        pair = swap(pair_sib)
        grad_rows = joined(gq_own, pair[1]).reshape(rows, head_cols)
        grad_rows, high, weight_own = lax.optimization_barrier((grad_rows, high, weight_own))
        weight_other = swap(weight_own)
        every_grad = lax.all_gather(grad_rows, "grp", axis=0, tiled=False)
    with jax.named_scope("return"):
        first = send(high, 3)
        terms, terms_sib = weight_terms(core_at, grad_rows, hidden_rows)
        first, terms, terms_sib = lax.optimization_barrier((first, terms, terms_sib))
        halved = combine_half("combine_high", mid, first, mid[0].shape[0])
        halved, terms, terms_sib = lax.optimization_barrier((halved, terms, terms_sib))
        second = send(halved, 2)
        terms = (terms.astype(F32) + swap(terms_sib).astype(F32)).astype(BF16)
        stays = combine_half("combine_low", low, first, 0)
        second, stays, terms = lax.optimization_barrier((second, stays, terms))
        *square, mine = combine_square(stays, second)
        square = [
            lax.ppermute(square[3 * pair + m], "chip", square_pairs(pair, m + 1))
            for pair in range(2)
            for m in range(3)
        ]
        square, mine, terms = lax.optimization_barrier((square, mine, terms))
        terms = lax.all_to_all(terms, "chip", split_axis=0, concat_axis=0, tiled=True)
        d_hidden = hidden_grads(core_at, every_grad, weight_own, weight_other)
        sums, sums_sib = combine_last(mine, square)
        other = swap(sums_sib)
        other, d_hidden = lax.optimization_barrier((other, d_hidden))
        d_keys = joined(sums[0], other[0])
        d_values = joined(sums[1], other[1])
        d_weight = weight_sum(terms)
        d_hidden = d_hidden.reshape(spans, span_len, wide)
    with jax.named_scope("context"):
        context = joined(ctx_own, pair[0])
    return context, d_hidden, d_keys, d_values, d_weight


def solution(mesh):
    fine = Mesh(mesh.devices.reshape(mesh.devices.shape[0], CHIPS, 2), ("grp", "chip", "core"))
    placed = (
        P(NB, None, None),
        P(None, "grp"),
        P(NB, None, "grp"),
        P(NB, None, "grp"),
        P(NB, None),
        P(NB),
        P(NB, None, "grp"),
    )
    return jax.shard_map(
        per_device,
        mesh=fine,
        in_specs=placed,
        out_specs=(
            P(NB, None, "grp"),
            P(NB, None, "grp"),
            P(NB, None, "grp"),
            P(NB, None, "grp"),
            P(NB, "grp"),
        ),
        check_vma=False,
    )
```

```python
import math

import jax
import jax.numpy as jnp
from jax import lax
from jax.experimental import pallas as pl
from jax.experimental.pallas import tpu as pltpu
from jax.sharding import Mesh, PartitionSpec as P

DH = 128
SIDE = 4
CHIPS = SIDE * SIDE
NB = ("chip", "core")
F32 = jnp.float32
BF16 = jnp.bfloat16
MIB = 2**20


def chip_pairs(move):
    pairs = []
    for x in range(SIDE):
        for y in range(SIDE):
            to_x, to_y = move(x, y)
            pairs.append((x * SIDE + y, to_x * SIDE + to_y))
    return pairs


LINKS = (
    chip_pairs(lambda x, y: (x ^ 1, y)),
    chip_pairs(lambda x, y: (x, y ^ 1)),
    chip_pairs(lambda x, y: (x ^ 3, y)),
    chip_pairs(lambda x, y: (x, y ^ 3)),
)


def cube_bits(chip):
    x, y = chip // SIDE, chip % SIDE
    return ((x ^ (x >> 1)) & 1, (y ^ (y >> 1)) & 1, x >> 1, y >> 1)


ORDERS = ((0, 1, 3, 2), (0, 1, 2, 3), (2, 3, 1, 0), (2, 3, 0, 1))


def cube_place(mine, chip, order):
    here, there = cube_bits(mine), cube_bits(chip)
    across = [a ^ b for a, b in zip(here, there)]
    return sum(across[d] << k for k, d in enumerate(order))


def square_pairs(pair, bits):
    moves = [dict(LINKS[d]) for k, d in enumerate(ORDERS[2 * pair][:2]) if bits >> k & 1]
    pairs = []
    for start in range(CHIPS):
        to = start
        for move in moves:
            to = move[to]
        pairs.append((start, to))
    return pairs


def swap(value):
    return lax.ppermute(value, "core", [(0, 1), (1, 0)])


def send(streams, k):
    return [lax.ppermute(h, "chip", LINKS[ORDERS[s][k]]) for s, h in enumerate(streams)]


def in_hbm(array):
    return pltpu.with_memory_space_constraint(array, pltpu.HBM)


def add_up(block, *refs):
    total = refs[0][block].astype(F32)
    for ref in refs[1:]:
        total = total + ref[block].astype(F32)
    return total


def half_body(kept, came, out, held, sem, offset):
    size = held.shape[1]
    loads = [pltpu.make_async_copy(kept[s], held.at[s], sem.at[s]) for s in range(4)]
    for copy in loads:
        copy.start()
    for s in range(4):
        loads[s].wait()

        def step(i, carry):
            total = held[s, i].astype(F32) + came[s][offset + i].astype(F32)
            out[s][i] = total.astype(BF16)
            return carry

        lax.fori_loop(0, size, step, 0, unroll=4)


def in_vmem(body, name, out_shape, *operands):
    vmem = pl.BlockSpec(memory_space=pltpu.VMEM)
    return pl.pallas_call(
        body,
        out_shape=out_shape,
        in_specs=[vmem] * len(operands),
        out_specs=[vmem] * len(out_shape),
        compiler_params=pltpu.CompilerParams(vmem_limit_bytes=6 * MIB),
        name=name,
    )(*operands)


def combine_half(name, kept, came, offset):
    def body(*refs):
        half_body(refs[:4], refs[4:8], refs[8:12], *refs[12:], offset)

    vmem = pl.BlockSpec(memory_space=pltpu.VMEM)
    return pl.pallas_call(
        body,
        out_shape=[jax.ShapeDtypeStruct(kept[0].shape, BF16)] * 4,
        in_specs=[pl.BlockSpec(memory_space=pl.ANY)] * 4 + [vmem] * 4,
        out_specs=[vmem] * 4,
        scratch_shapes=[pltpu.VMEM((4, *kept[0].shape), BF16), pltpu.SemaphoreType.DMA((4,))],
        compiler_params=pltpu.CompilerParams(vmem_limit_bytes=6 * MIB),
        name=name,
    )(*[in_hbm(k) for k in kept], *came)


def square_body(*refs):
    cut = refs[0].shape[0] // 4
    mine = refs[14]

    def step(i, carry):
        for s in range(4):
            for m in range(3):
                total = add_up((m + 1) * cut + i, refs[s], refs[4 + s])
                refs[8 + s // 2 * 3 + m][s % 2, i] = total.astype(BF16)
            mine[s, i] = add_up(i, refs[s], refs[4 + s])
        return carry

    lax.fori_loop(0, cut, step, 0)


def combine_square(kept, came):
    size, block_len, width = kept[0].shape
    shape = jax.ShapeDtypeStruct((2, size // 4, block_len, width), BF16)
    mine = jax.ShapeDtypeStruct((4, size // 4, block_len, width), F32)
    return in_vmem(square_body, "combine_square", [shape] * 6 + [mine], *kept, *came)


def last_body(mine_in, *refs):
    came, (out_own, out_sib), (mine, held, sem) = refs[:6], refs[6:8], refs[8:]
    loads = [pltpu.make_async_copy(mine_in, mine, sem.at[6])]
    for n in range(6):
        loads.append(pltpu.make_async_copy(came[n], held.at[n], sem.at[n]))
    for copy in loads:
        copy.start()
    for copy in loads:
        copy.wait()

    def step(i, carry):
        for s in range(4):
            pair = s // 2
            total = mine[s, i]
            for n in range(3 * pair, 3 * pair + 3):
                total = total + held[n, s % 2, i].astype(F32)
            (out_sib if s % 2 else out_own)[pair, i] = total.astype(BF16)
        return carry

    lax.fori_loop(0, mine.shape[1], step, 0)


def combine_last(mine, square):
    part = (2, *mine.shape[1:])
    left = pl.BlockSpec(memory_space=pl.ANY)
    vmem = pl.BlockSpec(memory_space=pltpu.VMEM)
    return pl.pallas_call(
        last_body,
        out_shape=[jax.ShapeDtypeStruct(part, BF16)] * 2,
        in_specs=[left] * 7,
        out_specs=[vmem] * 2,
        scratch_shapes=[
            pltpu.VMEM(mine.shape, F32),
            pltpu.VMEM((6, *part), BF16),
            pltpu.SemaphoreType.DMA((7,)),
        ],
        compiler_params=pltpu.CompilerParams(vmem_limit_bytes=6 * MIB),
        name="combine_last",
    )(mine, *[in_hbm(a) for a in square])


def square_join_body(*refs):
    cut = refs[0].shape[1]
    for s in range(4):
        for m in range(4):
            for i in range(cut):
                refs[8 + s][m * cut + i] = refs[2 * m + s // 2][s % 2, i]


def join_square(pairs, came):
    _, cut, block_len, width = pairs[0].shape
    shape = jax.ShapeDtypeStruct((4 * cut, block_len, width), BF16)
    return in_vmem(square_join_body, "join_square", [shape] * 4, *pairs, *came)


def join_body(*refs):
    held, came, out, sem = refs[:4], refs[4:8], refs[8:12], refs[12]
    size = held[0].shape[0]
    copies = []
    for s in range(4):
        for part, ref in enumerate((held[s], came[s])):
            to = out[s].at[pl.ds(part * size, size)]
            copies.append(pltpu.make_async_copy(ref, to, sem.at[2 * s + part]))
    for copy in copies:
        copy.start()
    for copy in copies:
        copy.wait()


def join_halves(held, came):
    shape = jax.ShapeDtypeStruct((2 * held[0].shape[0], *held[0].shape[1:]), BF16)
    left = pl.BlockSpec(memory_space=pl.ANY)
    return pl.pallas_call(
        join_body,
        out_shape=[shape] * 4,
        in_specs=[left] * 8,
        out_specs=[left] * 4,
        scratch_shapes=[pltpu.SemaphoreType.DMA((8,))],
        compiler_params=pltpu.CompilerParams(vmem_limit_bytes=MIB),
        name="join_halves",
    )(*held, *came)


def project_body(core, hid_ref, w_ref, own, other):
    scale = 1.0 / math.sqrt(DH)
    both = jnp.dot(hid_ref[...], w_ref[...], preferred_element_type=F32) * scale
    first, second = both[:, :DH].astype(BF16), both[:, DH:].astype(BF16)

    @pl.when(core[0] == 0)
    def _():
        own[...] = first
        other[...] = second

    @pl.when(core[0] != 0)
    def _():
        own[...] = second
        other[...] = first


def project(core, hidden_rows, query_weight):
    rows, model_width = hidden_rows.shape
    chunk = rows // 8
    out_spec = pl.BlockSpec((chunk, DH), lambda i, p: (i, 0))
    return pl.pallas_call(
        project_body,
        out_shape=[jax.ShapeDtypeStruct((rows, DH), BF16)] * 2,
        grid_spec=pltpu.PrefetchScalarGridSpec(
            num_scalar_prefetch=1,
            grid=(rows // chunk,),
            in_specs=[
                pl.BlockSpec((chunk, model_width), lambda i, p: (i, 0)),
                pl.BlockSpec(query_weight.shape, lambda i, p: (0, 0)),
            ],
            out_specs=[out_spec] * 2,
        ),
        compiler_params=pltpu.CompilerParams(vmem_limit_bytes=12 * MIB),
        name="project",
    )(core, in_hbm(hidden_rows), query_weight)


def weight_sum_body(terms, out):
    total = terms[0].astype(F32)
    for n in range(1, terms.shape[0]):
        total = total + terms[n].astype(F32)
    out[...] = total.T.astype(BF16)


def weight_sum(terms):
    _, head_cols, part = terms.shape
    shape = jax.ShapeDtypeStruct((part, head_cols), BF16)
    return in_vmem(weight_sum_body, "weight_sum", [shape], terms)[0]


def attention_body(
    slots, counts, q_own, q_sib, g_own, g_sib, *refs
):
    kv_in, (ctx_own, gq_own, pair_sib), outs = refs[:8], refs[8:11], refs[11:23]
    kv_all, dk_all, dv_all, in_sem, out_sem = refs[23:]
    scale = 1.0 / math.sqrt(DH)
    block_len = kv_all.shape[1]
    half = dk_all.shape[0] // 4
    loads = []
    for n, ref in enumerate(kv_in):
        part = kv_all.at[pl.ds(n * half, half)]
        loads.append(pltpu.make_async_copy(ref, part, in_sem.at[n]))
    for copy in loads:
        copy.start()
    blank = jnp.zeros(dk_all.shape[1:], BF16)

    def clear(n, carry):
        dk_all[n] = blank
        dv_all[n] = blank
        return carry

    lax.fori_loop(0, dk_all.shape[0], clear, 0, unroll=4)
    for copy in loads:
        copy.wait()
    spans = q_own.shape[0]
    rows = (((1,), (1,)), ((), ()))
    cols = (((0,), (0,)), ((), ()))

    def step(i, carry):
        batch = [(q_own, g_own, i, i), (q_sib, g_sib, i, i + spans)]
        q = [qr[n] for qr, _, n, _ in batch]
        g = [gr[n] for _, gr, n, _ in batch]
        refs = [(2 * span, 2 * span + 1) for _, _, _, span in batch]
        k = [jnp.concatenate([kv_all[slots[0, r]] for r in pair], axis=0) for pair in refs]
        v = [jnp.concatenate([kv_all[slots[1, r]] for r in pair], axis=0) for pair in refs]
        s = [lax.dot_general(a, b, rows, preferred_element_type=F32) for a, b in zip(q, k)]
        ga = [lax.dot_general(a, b, rows, preferred_element_type=F32) for a, b in zip(g, v)]
        place = lax.broadcasted_iota(jnp.int32, s[0].shape, 1)
        s = [
            jnp.where(place < counts[span] * block_len, a, -jnp.inf)
            for a, (_, _, _, span) in zip(s, batch)
        ]
        w = [jnp.exp(a - jnp.max(a, axis=1, keepdims=True)) for a in s]
        att = [a / jnp.sum(a, axis=1, keepdims=True) for a in w]
        low = [a.astype(BF16) for a in att]
        gs = [
            (a * (b - jnp.sum(a * b, axis=1, keepdims=True))).astype(BF16)
            for a, b in zip(att, ga)
        ]
        ctx = [jnp.dot(a, b, preferred_element_type=F32).astype(BF16) for a, b in zip(low, v)]
        gq = [(jnp.dot(a, b, preferred_element_type=F32) * scale).astype(BF16) for a, b in zip(gs, k)]
        dk = [lax.dot_general(a, b, cols, preferred_element_type=F32).astype(BF16) for a, b in zip(gs, q)]
        dv = [lax.dot_general(a, b, cols, preferred_element_type=F32).astype(BF16) for a, b in zip(low, g)]
        ctx_own[i] = ctx[0]
        gq_own[i] = gq[0]
        pair_sib[0, i] = ctx[1]
        pair_sib[1, i] = gq[1]
        for n, pair in enumerate(refs):
            for j, r in enumerate(pair):
                at = slots[2, r]
                part = dk[n][j * block_len : (j + 1) * block_len].astype(F32)
                dk_all[at] = (dk_all[at].astype(F32) + part).astype(BF16)
                at = slots[3, r]
                part = dv[n][j * block_len : (j + 1) * block_len].astype(F32)
                dv_all[at] = (dv_all[at].astype(F32) + part).astype(BF16)
        return carry

    lax.fori_loop(0, spans, step, 0, unroll=2)
    stores = []
    for s in range(4):
        whole = dk_all if s < 2 else dv_all
        at = s % 2 * 2 * half
        for ref in outs[3 * s : 3 * s + 3]:
            size = ref.shape[0]
            stores.append(
                pltpu.make_async_copy(whole.at[pl.ds(at, size)], ref, out_sem.at[len(stores)])
            )
            at += size
    for copy in stores:
        copy.start()
    for copy in stores:
        copy.wait()


def attention(slots, counts, q_own, q_sib, g_own, g_sib, gathered):
    spans, span_len, width = q_own.shape
    half, block_len, _ = gathered[0].shape
    small = jax.ShapeDtypeStruct((spans, span_len, width), BF16)
    pair = jax.ShapeDtypeStruct((2, spans, span_len, width), BF16)
    pieces = [half // 2, half // 2, half] * 4
    large = [pltpu.HBM((n, block_len, width), BF16) for n in pieces]
    grads = pltpu.VMEM((4 * half, block_len, width), BF16)
    smem = pl.BlockSpec(memory_space=pltpu.SMEM)
    vmem = pl.BlockSpec(memory_space=pltpu.VMEM)
    hbm = pl.BlockSpec(memory_space=pltpu.HBM)
    left = pl.BlockSpec(memory_space=pl.ANY)
    return pl.pallas_call(
        attention_body,
        out_shape=[small, small, pair] + large,
        in_specs=[smem] * 2 + [vmem] * 4 + [left] * 8,
        out_specs=[vmem] * 3 + [hbm] * 12,
        scratch_shapes=[
            pltpu.VMEM((8 * half, block_len, width), BF16),
            grads,
            grads,
            pltpu.SemaphoreType.DMA((8,)),
            pltpu.SemaphoreType.DMA((12,)),
        ],
        compiler_params=pltpu.CompilerParams(vmem_limit_bytes=20 * MIB),
        name="attention",
    )(slots, counts, q_own, q_sib, g_own, g_sib, *gathered)


def weight_body(core, gq_ref, hid_ref, own, sib, gq_t):
    step = pl.program_id(0)

    @pl.when(step == 0)
    def _():
        gq_t[...] = gq_ref[...].T

    term = jnp.dot(gq_t[...], hid_ref[...], preferred_element_type=F32).astype(BF16)
    chips, _, part = own.shape
    for n in range(chips):
        even = term[:, 2 * n * part : (2 * n + 1) * part]
        odd = term[:, (2 * n + 1) * part : (2 * n + 2) * part]

        @pl.when(core[0] == 0)
        def _():
            own[n] = even
            sib[n] = odd

        @pl.when(core[0] != 0)
        def _():
            own[n] = odd
            sib[n] = even


def weight_terms(core, grad_rows, hidden_rows):
    rows, model_width = hidden_rows.shape
    head_cols = grad_rows.shape[1]
    part = model_width // (2 * CHIPS)
    chips = 2
    wide = 2 * chips * part
    out_spec = pl.BlockSpec((chips, head_cols, part), lambda i, p: (i, 0, 0))
    return pl.pallas_call(
        weight_body,
        out_shape=[jax.ShapeDtypeStruct((CHIPS, head_cols, part), BF16)] * 2,
        grid_spec=pltpu.PrefetchScalarGridSpec(
            num_scalar_prefetch=1,
            grid=(CHIPS // chips,),
            in_specs=[
                pl.BlockSpec(grad_rows.shape, lambda i, p: (0, 0)),
                pl.BlockSpec((rows, wide), lambda i, p: (0, i)),
            ],
            out_specs=[out_spec] * 2,
            scratch_shapes=[pltpu.VMEM(grad_rows.shape[::-1], BF16)],
        ),
        compiler_params=pltpu.CompilerParams(vmem_limit_bytes=12 * MIB),
        name="weight_terms",
    )(core, grad_rows, in_hbm(hidden_rows))


def hidden_body(core, gq_ref, mine, other, out):
    wide = mine.shape[1]
    for n, w_ref in enumerate((mine, other)):
        total = None
        for g in range(gq_ref.shape[0]):
            term = lax.dot_general(
                gq_ref[g], w_ref[g], (((1,), (1,)), ((), ())), preferred_element_type=F32
            )
            term = term.astype(BF16).astype(F32)
            total = term if total is None else total + term
        at = pl.multiple_of((core[0] if n == 0 else 1 - core[0]) * wide, wide)
        out[:, pl.ds(at, wide)] = total.astype(BF16)


def hidden_grads(core, every_grad, mine, other):
    groups, rows, head_cols = every_grad.shape
    wide = 2 * mine.shape[1]
    chunk = rows // 4
    return pl.pallas_call(
        hidden_body,
        out_shape=jax.ShapeDtypeStruct((rows, wide), BF16),
        grid_spec=pltpu.PrefetchScalarGridSpec(
            num_scalar_prefetch=1,
            grid=(rows // chunk,),
            in_specs=[
                pl.BlockSpec((groups, chunk, head_cols), lambda i, p: (0, i, 0)),
                pl.BlockSpec(mine.shape, lambda i, p: (0, 0, 0)),
                pl.BlockSpec(mine.shape, lambda i, p: (0, 0, 0)),
            ],
            out_specs=pl.BlockSpec((chunk, wide), lambda i, p: (i, 0)),
        ),
        compiler_params=pltpu.CompilerParams(vmem_limit_bytes=16 * MIB),
        name="hidden_grads",
    )(core, in_hbm(every_grad), mine, other)


def per_device(hidden, query_weight, keys, values, neighbour_ids, neighbour_counts, d_context):
    spans, span_len, model_width = hidden.shape
    blocks, block_len, head_cols = keys.shape
    groups = lax.axis_size("grp")
    chip = lax.axis_index("chip")
    core = lax.axis_index("core")
    core_at = core.reshape(1)
    rows = spans * span_len
    refs = neighbour_ids.size

    def both(array):
        first, second = array[..., :DH], array[..., DH:]
        return jnp.where(core == 0, first, second), jnp.where(core == 0, second, first)

    def joined(own, other):
        return jnp.where(
            core == 0,
            jnp.concatenate([own, other], axis=-1),
            jnp.concatenate([other, own], axis=-1),
        )

    with jax.named_scope("gather"):
        own, other = both(jnp.stack([keys, values]))
        came = swap(other)
        pairs = lax.optimization_barrier(
            [jnp.stack([own[0], came[0]]), jnp.stack([own[1], came[1]])]
        )

        def across(pieces, k):
            return [lax.ppermute(p, "chip", LINKS[ORDERS[s][k]]) for s, p in enumerate(pieces)]

        came = [
            lax.ppermute(pairs[pair], "chip", square_pairs(pair, m))
            for m in (1, 2, 3)
            for pair in range(2)
        ]
        held = join_square(pairs, came)
        held = join_halves(held, across(held, 2))
        last = across(held, 3)
    with jax.named_scope("queries"):
        hidden_rows = hidden.reshape(rows, model_width)
        query_own, query_other = project(core_at, hidden_rows, query_weight)
        query_own, query_other, leaving = lax.optimization_barrier(
            (query_own, query_other, query_weight)
        )
        last, query_own, query_other = lax.optimization_barrier((last, query_own, query_other))
        gathered = [part for parts in zip(held, last) for part in parts]
        query_own = query_own.reshape(spans, span_len, DH)
        query_sib = swap(query_other.reshape(spans, span_len, DH))
    with jax.named_scope("weight_rows"):
        wide = model_width // groups
        asked = leaving.reshape(groups, 2, wide // 2, head_cols)
        asked = jnp.where(core == 0, asked[:, 0], asked[:, 1])
        weight_own = lax.all_to_all(asked, "grp", split_axis=0, concat_axis=0, tiled=True)
    with jax.named_scope("more"):
        grad_own, grad_other = both(d_context)
        grad_sib = swap(grad_other)
    with jax.named_scope("slots"):
        table = jnp.concatenate([neighbour_ids.reshape(-1), neighbour_counts])
        table_sib = swap(table)
        ids = jnp.concatenate([table[:refs], table_sib[:refs]])
        counts = jnp.concatenate([table[refs:], table_sib[refs:]])
        owner, local = ids // blocks, ids % blocks
        far = jnp.where(owner % 2 == core, 0, 1)
        host = owner // 2

        def slot(orders, first):
            near_place = cube_place(chip, host, orders[0])
            far_place = CHIPS + cube_place(chip, host, orders[1])
            return (first + jnp.where(far == 0, near_place, far_place)) * blocks + local

        slots = jnp.stack(
            [
                slot(ORDERS[:2], 0),
                slot(ORDERS[2:], 2 * CHIPS),
                slot(ORDERS[:2], 0),
                slot(ORDERS[2:], 0),
            ]
        )
    with jax.named_scope("attend"):
        out = attention(slots, counts, query_own, query_sib, grad_own, grad_sib, gathered)
        ctx_own, gq_own, pair_sib = out[:3]
        low, mid, high = out[3::3], out[4::3], out[5::3]
    with jax.named_scope("grad_queries"):
        pair = swap(pair_sib)
        grad_rows = joined(gq_own, pair[1]).reshape(rows, head_cols)
        grad_rows, high, weight_own = lax.optimization_barrier((grad_rows, high, weight_own))
        weight_other = swap(weight_own)
        every_grad = lax.all_gather(grad_rows, "grp", axis=0, tiled=False)
    with jax.named_scope("return"):
        first = send(high, 3)
        terms, terms_sib = weight_terms(core_at, grad_rows, hidden_rows)
        context = joined(ctx_own, pair[0])
        first, terms, terms_sib, context = lax.optimization_barrier((first, terms, terms_sib, context))
        halved = combine_half("combine_high", mid, first, mid[0].shape[0])
        halved, terms, terms_sib = lax.optimization_barrier((halved, terms, terms_sib))
        second = send(halved, 2)
        terms = (terms.astype(F32) + swap(terms_sib).astype(F32)).astype(BF16)
        stays = combine_half("combine_low", low, first, 0)
        second, stays, terms = lax.optimization_barrier((second, stays, terms))
        *square, mine = combine_square(stays, second)
        square = [
            lax.ppermute(square[3 * pair + m], "chip", square_pairs(pair, m + 1))
            for pair in range(2)
            for m in range(3)
        ]
        square, mine, terms = lax.optimization_barrier((square, mine, terms))
        terms = lax.all_to_all(terms, "chip", split_axis=0, concat_axis=0, tiled=True)
        d_hidden = hidden_grads(core_at, every_grad, weight_own, weight_other)
        sums, sums_sib = combine_last(mine, square)
        other = swap(sums_sib)
        other, d_hidden = lax.optimization_barrier((other, d_hidden))
        d_hidden, terms = lax.optimization_barrier((d_hidden, terms))
        d_keys = joined(sums[0], other[0])
        d_values = joined(sums[1], other[1])
        d_weight = weight_sum(terms)
        d_hidden = d_hidden.reshape(spans, span_len, wide)
    return context, d_hidden, d_keys, d_values, d_weight


def solution(mesh):
    fine = Mesh(mesh.devices.reshape(mesh.devices.shape[0], CHIPS, 2), ("grp", "chip", "core"))
    placed = (
        P(NB, None, None),
        P(None, "grp"),
        P(NB, None, "grp"),
        P(NB, None, "grp"),
        P(NB, None),
        P(NB),
        P(NB, None, "grp"),
    )
    return jax.shard_map(
        per_device,
        mesh=fine,
        in_specs=placed,
        out_specs=(
            P(NB, None, "grp"),
            P(NB, None, "grp"),
            P(NB, None, "grp"),
            P(NB, None, "grp"),
            P(NB, "grp"),
        ),
        check_vma=False,
    )
```

```python
import math

import jax
import jax.numpy as jnp
from jax import lax
from jax.experimental import pallas as pl
from jax.experimental.pallas import tpu as pltpu
from jax.sharding import Mesh, PartitionSpec as P

DH = 128
SIDE = 4
CHIPS = SIDE * SIDE
NB = ("chip", "core")
F32 = jnp.float32
BF16 = jnp.bfloat16
MIB = 2**20


def chip_pairs(move):
    pairs = []
    for x in range(SIDE):
        for y in range(SIDE):
            to_x, to_y = move(x, y)
            pairs.append((x * SIDE + y, to_x * SIDE + to_y))
    return pairs


LINKS = (
    chip_pairs(lambda x, y: (x ^ 1, y)),
    chip_pairs(lambda x, y: (x, y ^ 1)),
    chip_pairs(lambda x, y: (x ^ 3, y)),
    chip_pairs(lambda x, y: (x, y ^ 3)),
)


def cube_bits(chip):
    x, y = chip // SIDE, chip % SIDE
    return ((x ^ (x >> 1)) & 1, (y ^ (y >> 1)) & 1, x >> 1, y >> 1)


ORDERS = ((0, 1, 3, 2), (0, 1, 2, 3), (2, 3, 1, 0), (2, 3, 0, 1))


def cube_place(mine, chip, order):
    here, there = cube_bits(mine), cube_bits(chip)
    across = [a ^ b for a, b in zip(here, there)]
    return sum(across[d] << k for k, d in enumerate(order))


def square_pairs(pair, bits):
    moves = [dict(LINKS[d]) for k, d in enumerate(ORDERS[2 * pair][:2]) if bits >> k & 1]
    pairs = []
    for start in range(CHIPS):
        to = start
        for move in moves:
            to = move[to]
        pairs.append((start, to))
    return pairs


def swap(value):
    return lax.ppermute(value, "core", [(0, 1), (1, 0)])


def send(streams, k):
    return [lax.ppermute(h, "chip", LINKS[ORDERS[s][k]]) for s, h in enumerate(streams)]


def in_hbm(array):
    return pltpu.with_memory_space_constraint(array, pltpu.HBM)


def add_up(block, *refs):
    total = refs[0][block].astype(F32)
    for ref in refs[1:]:
        total = total + ref[block].astype(F32)
    return total


def half_body(kept, came, out, held, sem, offset):
    size = held.shape[1]
    loads = [pltpu.make_async_copy(kept[s], held.at[s], sem.at[s]) for s in range(4)]
    for copy in loads:
        copy.start()
    for s in range(4):
        loads[s].wait()

        def step(i, carry):
            total = held[s, i].astype(F32) + came[s][offset + i].astype(F32)
            out[s][i] = total.astype(BF16)
            return carry

        lax.fori_loop(0, size, step, 0, unroll=4)


def in_vmem(body, name, out_shape, *operands):
    vmem = pl.BlockSpec(memory_space=pltpu.VMEM)
    return pl.pallas_call(
        body,
        out_shape=out_shape,
        in_specs=[vmem] * len(operands),
        out_specs=[vmem] * len(out_shape),
        compiler_params=pltpu.CompilerParams(vmem_limit_bytes=6 * MIB),
        name=name,
    )(*operands)


def combine_half(name, kept, came, offset):
    def body(*refs):
        half_body(refs[:4], refs[4:8], refs[8:12], *refs[12:], offset)

    vmem = pl.BlockSpec(memory_space=pltpu.VMEM)
    return pl.pallas_call(
        body,
        out_shape=[jax.ShapeDtypeStruct(kept[0].shape, BF16)] * 4,
        in_specs=[pl.BlockSpec(memory_space=pl.ANY)] * 4 + [vmem] * 4,
        out_specs=[vmem] * 4,
        scratch_shapes=[pltpu.VMEM((4, *kept[0].shape), BF16), pltpu.SemaphoreType.DMA((4,))],
        compiler_params=pltpu.CompilerParams(vmem_limit_bytes=6 * MIB),
        name=name,
    )(*[in_hbm(k) for k in kept], *came)


def square_body(*refs):
    cut = refs[0].shape[0] // 4
    mine = refs[14]

    def step(i, carry):
        for s in range(4):
            for m in range(3):
                total = add_up((m + 1) * cut + i, refs[s], refs[4 + s])
                refs[8 + s // 2 * 3 + m][s % 2, i] = total.astype(BF16)
            mine[s, i] = add_up(i, refs[s], refs[4 + s])
        return carry

    lax.fori_loop(0, cut, step, 0)


def combine_square(kept, came):
    size, block_len, width = kept[0].shape
    shape = jax.ShapeDtypeStruct((2, size // 4, block_len, width), BF16)
    mine = jax.ShapeDtypeStruct((4, size // 4, block_len, width), F32)
    return in_vmem(square_body, "combine_square", [shape] * 6 + [mine], *kept, *came)


def last_body(mine_in, *refs):
    came, (out_own, out_sib), (mine, held, sem) = refs[:6], refs[6:8], refs[8:]
    loads = [pltpu.make_async_copy(mine_in, mine, sem.at[6])]
    for n in range(6):
        loads.append(pltpu.make_async_copy(came[n], held.at[n], sem.at[n]))
    for copy in loads:
        copy.start()
    for copy in loads:
        copy.wait()

    def step(i, carry):
        for s in range(4):
            pair = s // 2
            total = mine[s, i]
            for n in range(3 * pair, 3 * pair + 3):
                total = total + held[n, s % 2, i].astype(F32)
            (out_sib if s % 2 else out_own)[pair, i] = total.astype(BF16)
        return carry

    lax.fori_loop(0, mine.shape[1], step, 0)


def combine_last(mine, square):
    part = (2, *mine.shape[1:])
    left = pl.BlockSpec(memory_space=pl.ANY)
    vmem = pl.BlockSpec(memory_space=pltpu.VMEM)
    return pl.pallas_call(
        last_body,
        out_shape=[jax.ShapeDtypeStruct(part, BF16)] * 2,
        in_specs=[left] * 7,
        out_specs=[vmem] * 2,
        scratch_shapes=[
            pltpu.VMEM(mine.shape, F32),
            pltpu.VMEM((6, *part), BF16),
            pltpu.SemaphoreType.DMA((7,)),
        ],
        compiler_params=pltpu.CompilerParams(vmem_limit_bytes=6 * MIB),
        name="combine_last",
    )(*[in_hbm(a) for a in (mine, *square)])


def square_join_body(*refs):
    cut = refs[0].shape[1]
    for s in range(4):
        for m in range(4):
            for i in range(cut):
                refs[8 + s][m * cut + i] = refs[2 * m + s // 2][s % 2, i]


def join_square(pairs, came):
    _, cut, block_len, width = pairs[0].shape
    shape = jax.ShapeDtypeStruct((4 * cut, block_len, width), BF16)
    return in_vmem(square_join_body, "join_square", [shape] * 4, *pairs, *came)


def join_body(*refs):
    size = refs[0].shape[0]

    def step(i, carry):
        for s in range(4):
            refs[8 + s][i] = refs[s][i]
            refs[8 + s][size + i] = refs[4 + s][i]
        return carry

    lax.fori_loop(0, size, step, 0, unroll=2)


def join_halves(held, came):
    shape = jax.ShapeDtypeStruct((2 * held[0].shape[0], *held[0].shape[1:]), BF16)
    return in_vmem(join_body, "join_halves", [shape] * 4, *held, *came)


def project_body(core, hid_ref, w_ref, own, other):
    scale = 1.0 / math.sqrt(DH)
    both = jnp.dot(hid_ref[...], w_ref[...], preferred_element_type=F32) * scale
    first, second = both[:, :DH].astype(BF16), both[:, DH:].astype(BF16)

    @pl.when(core[0] == 0)
    def _():
        own[...] = first
        other[...] = second

    @pl.when(core[0] != 0)
    def _():
        own[...] = second
        other[...] = first


def project(core, hidden_rows, query_weight):
    rows, model_width = hidden_rows.shape
    chunk = rows // 8
    out_spec = pl.BlockSpec((chunk, DH), lambda i, p: (i, 0))
    return pl.pallas_call(
        project_body,
        out_shape=[jax.ShapeDtypeStruct((rows, DH), BF16)] * 2,
        grid_spec=pltpu.PrefetchScalarGridSpec(
            num_scalar_prefetch=1,
            grid=(rows // chunk,),
            in_specs=[
                pl.BlockSpec((chunk, model_width), lambda i, p: (i, 0)),
                pl.BlockSpec(query_weight.shape, lambda i, p: (0, 0)),
            ],
            out_specs=[out_spec] * 2,
        ),
        compiler_params=pltpu.CompilerParams(vmem_limit_bytes=12 * MIB),
        name="project",
    )(core, in_hbm(hidden_rows), query_weight)


def weight_sum_body(terms, out):
    total = terms[0].astype(F32)
    for n in range(1, terms.shape[0]):
        total = total + terms[n].astype(F32)
    out[...] = total.T.astype(BF16)


def weight_sum(terms):
    _, head_cols, part = terms.shape
    shape = jax.ShapeDtypeStruct((part, head_cols), BF16)
    return in_vmem(weight_sum_body, "weight_sum", [shape], terms)[0]


def attention_body(
    slots, counts, q_own, q_sib, g_own, g_sib, *refs
):
    kv_in, (ctx_own, gq_own, pair_sib), outs = refs[:8], refs[8:11], refs[11:23]
    kv_all, dk_all, dv_all, in_sem, out_sem = refs[23:]
    scale = 1.0 / math.sqrt(DH)
    block_len = kv_all.shape[1]
    half = dk_all.shape[0] // 4
    loads = []
    for n, ref in enumerate(kv_in):
        part = kv_all.at[pl.ds(n * half, half)]
        loads.append(pltpu.make_async_copy(ref, part, in_sem.at[n]))
    for copy in loads:
        copy.start()
    blank = jnp.zeros(dk_all.shape[1:], BF16)

    def clear(n, carry):
        dk_all[n] = blank
        dv_all[n] = blank
        return carry

    lax.fori_loop(0, dk_all.shape[0], clear, 0, unroll=4)
    for copy in loads:
        copy.wait()
    spans = q_own.shape[0]
    rows = (((1,), (1,)), ((), ()))
    cols = (((0,), (0,)), ((), ()))

    def step(i, carry):
        batch = [(q_own, g_own, i, i), (q_sib, g_sib, i, i + spans)]
        q = [qr[n] for qr, _, n, _ in batch]
        g = [gr[n] for _, gr, n, _ in batch]
        refs = [(2 * span, 2 * span + 1) for _, _, _, span in batch]
        k = [jnp.concatenate([kv_all[slots[0, r]] for r in pair], axis=0) for pair in refs]
        v = [jnp.concatenate([kv_all[slots[1, r]] for r in pair], axis=0) for pair in refs]
        s = [lax.dot_general(a, b, rows, preferred_element_type=F32) for a, b in zip(q, k)]
        ga = [lax.dot_general(a, b, rows, preferred_element_type=F32) for a, b in zip(g, v)]
        place = lax.broadcasted_iota(jnp.int32, s[0].shape, 1)
        s = [
            jnp.where(place < counts[span] * block_len, a, -jnp.inf)
            for a, (_, _, _, span) in zip(s, batch)
        ]
        w = [jnp.exp(a - jnp.max(a, axis=1, keepdims=True)) for a in s]
        att = [a / jnp.sum(a, axis=1, keepdims=True) for a in w]
        low = [a.astype(BF16) for a in att]
        gs = [
            (a * (b - jnp.sum(a * b, axis=1, keepdims=True))).astype(BF16)
            for a, b in zip(att, ga)
        ]
        ctx = [jnp.dot(a, b, preferred_element_type=F32).astype(BF16) for a, b in zip(low, v)]
        gq = [(jnp.dot(a, b, preferred_element_type=F32) * scale).astype(BF16) for a, b in zip(gs, k)]
        dk = [lax.dot_general(a, b, cols, preferred_element_type=F32).astype(BF16) for a, b in zip(gs, q)]
        dv = [lax.dot_general(a, b, cols, preferred_element_type=F32).astype(BF16) for a, b in zip(low, g)]
        ctx_own[i] = ctx[0]
        gq_own[i] = gq[0]
        pair_sib[0, i] = ctx[1]
        pair_sib[1, i] = gq[1]
        for n, pair in enumerate(refs):
            for j, r in enumerate(pair):
                at = slots[2, r]
                part = dk[n][j * block_len : (j + 1) * block_len].astype(F32)
                dk_all[at] = (dk_all[at].astype(F32) + part).astype(BF16)
                at = slots[3, r]
                part = dv[n][j * block_len : (j + 1) * block_len].astype(F32)
                dv_all[at] = (dv_all[at].astype(F32) + part).astype(BF16)
        return carry

    lax.fori_loop(0, spans, step, 0, unroll=2)
    stores = []
    for s in range(4):
        whole = dk_all if s < 2 else dv_all
        at = s % 2 * 2 * half
        for ref in outs[3 * s : 3 * s + 3]:
            size = ref.shape[0]
            stores.append(
                pltpu.make_async_copy(whole.at[pl.ds(at, size)], ref, out_sem.at[len(stores)])
            )
            at += size
    for copy in stores:
        copy.start()
    for copy in stores:
        copy.wait()


def attention(slots, counts, q_own, q_sib, g_own, g_sib, gathered):
    spans, span_len, width = q_own.shape
    half, block_len, _ = gathered[0].shape
    small = jax.ShapeDtypeStruct((spans, span_len, width), BF16)
    pair = jax.ShapeDtypeStruct((2, spans, span_len, width), BF16)
    pieces = [half // 2, half // 2, half] * 4
    large = [pltpu.HBM((n, block_len, width), BF16) for n in pieces]
    grads = pltpu.VMEM((4 * half, block_len, width), BF16)
    smem = pl.BlockSpec(memory_space=pltpu.SMEM)
    vmem = pl.BlockSpec(memory_space=pltpu.VMEM)
    hbm = pl.BlockSpec(memory_space=pltpu.HBM)
    left = pl.BlockSpec(memory_space=pl.ANY)
    return pl.pallas_call(
        attention_body,
        out_shape=[small, small, pair] + large,
        in_specs=[smem] * 2 + [vmem] * 4 + [left] * 8,
        out_specs=[vmem] * 3 + [hbm] * 12,
        scratch_shapes=[
            pltpu.VMEM((8 * half, block_len, width), BF16),
            grads,
            grads,
            pltpu.SemaphoreType.DMA((8,)),
            pltpu.SemaphoreType.DMA((12,)),
        ],
        compiler_params=pltpu.CompilerParams(vmem_limit_bytes=20 * MIB),
        name="attention",
    )(slots, counts, q_own, q_sib, g_own, g_sib, *[in_hbm(a) for a in gathered])


def weight_body(core, gq_ref, hid_ref, own, sib, gq_t):
    step = pl.program_id(0)

    @pl.when(step == 0)
    def _():
        gq_t[...] = gq_ref[...].T

    term = jnp.dot(gq_t[...], hid_ref[...], preferred_element_type=F32).astype(BF16)
    chips, _, part = own.shape
    for n in range(chips):
        even = term[:, 2 * n * part : (2 * n + 1) * part]
        odd = term[:, (2 * n + 1) * part : (2 * n + 2) * part]

        @pl.when(core[0] == 0)
        def _():
            own[n] = even
            sib[n] = odd

        @pl.when(core[0] != 0)
        def _():
            own[n] = odd
            sib[n] = even


def weight_terms(core, grad_rows, hidden_rows):
    rows, model_width = hidden_rows.shape
    head_cols = grad_rows.shape[1]
    part = model_width // (2 * CHIPS)
    chips = 2
    wide = 2 * chips * part
    out_spec = pl.BlockSpec((chips, head_cols, part), lambda i, p: (i, 0, 0))
    return pl.pallas_call(
        weight_body,
        out_shape=[jax.ShapeDtypeStruct((CHIPS, head_cols, part), BF16)] * 2,
        grid_spec=pltpu.PrefetchScalarGridSpec(
            num_scalar_prefetch=1,
            grid=(CHIPS // chips,),
            in_specs=[
                pl.BlockSpec(grad_rows.shape, lambda i, p: (0, 0)),
                pl.BlockSpec((rows, wide), lambda i, p: (0, i)),
            ],
            out_specs=[out_spec] * 2,
            scratch_shapes=[pltpu.VMEM(grad_rows.shape[::-1], BF16)],
        ),
        compiler_params=pltpu.CompilerParams(vmem_limit_bytes=12 * MIB),
        name="weight_terms",
    )(core, grad_rows, in_hbm(hidden_rows))


def hidden_body(core, gq_ref, mine, other, out):
    wide = mine.shape[1]
    for n, w_ref in enumerate((mine, other)):
        total = None
        for g in range(gq_ref.shape[0]):
            term = lax.dot_general(
                gq_ref[g], w_ref[g], (((1,), (1,)), ((), ())), preferred_element_type=F32
            )
            term = term.astype(BF16).astype(F32)
            total = term if total is None else total + term
        at = pl.multiple_of((core[0] if n == 0 else 1 - core[0]) * wide, wide)
        out[:, pl.ds(at, wide)] = total.astype(BF16)


def hidden_grads(core, every_grad, mine, other):
    groups, rows, head_cols = every_grad.shape
    wide = 2 * mine.shape[1]
    chunk = rows // 4
    return pl.pallas_call(
        hidden_body,
        out_shape=jax.ShapeDtypeStruct((rows, wide), BF16),
        grid_spec=pltpu.PrefetchScalarGridSpec(
            num_scalar_prefetch=1,
            grid=(rows // chunk,),
            in_specs=[
                pl.BlockSpec((groups, chunk, head_cols), lambda i, p: (0, i, 0)),
                pl.BlockSpec(mine.shape, lambda i, p: (0, 0, 0)),
                pl.BlockSpec(mine.shape, lambda i, p: (0, 0, 0)),
            ],
            out_specs=pl.BlockSpec((chunk, wide), lambda i, p: (i, 0)),
        ),
        compiler_params=pltpu.CompilerParams(vmem_limit_bytes=16 * MIB),
        name="hidden_grads",
    )(core, in_hbm(every_grad), mine, other)


def per_device(hidden, query_weight, keys, values, neighbour_ids, neighbour_counts, d_context):
    spans, span_len, model_width = hidden.shape
    blocks, block_len, head_cols = keys.shape
    groups = lax.axis_size("grp")
    chip = lax.axis_index("chip")
    core = lax.axis_index("core")
    core_at = core.reshape(1)
    rows = spans * span_len
    refs = neighbour_ids.size

    def both(array):
        first, second = array[..., :DH], array[..., DH:]
        return jnp.where(core == 0, first, second), jnp.where(core == 0, second, first)

    def joined(own, other):
        return jnp.where(
            core == 0,
            jnp.concatenate([own, other], axis=-1),
            jnp.concatenate([other, own], axis=-1),
        )

    with jax.named_scope("gather"):
        own, other = both(jnp.stack([keys, values]))
        came = swap(other)
        pairs = lax.optimization_barrier(
            [jnp.stack([own[0], came[0]]), jnp.stack([own[1], came[1]])]
        )

        def across(pieces, k):
            return [lax.ppermute(p, "chip", LINKS[ORDERS[s][k]]) for s, p in enumerate(pieces)]

        came = [
            lax.ppermute(pairs[pair], "chip", square_pairs(pair, m))
            for m in (1, 2, 3)
            for pair in range(2)
        ]
        held = join_square(pairs, came)
        held = join_halves(held, across(held, 2))
        last = across(held, 3)
    with jax.named_scope("queries"):
        hidden_rows = hidden.reshape(rows, model_width)
        query_own, query_other = project(core_at, hidden_rows, query_weight)
        query_own, query_other, leaving = lax.optimization_barrier(
            (query_own, query_other, query_weight)
        )
        last, query_own, query_other = lax.optimization_barrier((last, query_own, query_other))
        gathered = [part for parts in zip(held, last) for part in parts]
        query_own = query_own.reshape(spans, span_len, DH)
        query_sib = swap(query_other.reshape(spans, span_len, DH))
    with jax.named_scope("weight_rows"):
        wide = model_width // groups
        asked = leaving.reshape(groups, 2, wide // 2, head_cols)
        asked = jnp.where(core == 0, asked[:, 0], asked[:, 1])
        weight_own = lax.all_to_all(asked, "grp", split_axis=0, concat_axis=0, tiled=True)
    with jax.named_scope("more"):
        grad_own, grad_other = both(d_context)
        grad_sib = swap(grad_other)
    with jax.named_scope("slots"):
        table = jnp.concatenate([neighbour_ids.reshape(-1), neighbour_counts])
        table_sib = swap(table)
        ids = jnp.concatenate([table[:refs], table_sib[:refs]])
        counts = jnp.concatenate([table[refs:], table_sib[refs:]])
        owner, local = ids // blocks, ids % blocks
        far = jnp.where(owner % 2 == core, 0, 1)
        host = owner // 2

        def slot(orders, first):
            near_place = cube_place(chip, host, orders[0])
            far_place = CHIPS + cube_place(chip, host, orders[1])
            return (first + jnp.where(far == 0, near_place, far_place)) * blocks + local

        slots = jnp.stack(
            [
                slot(ORDERS[:2], 0),
                slot(ORDERS[2:], 2 * CHIPS),
                slot(ORDERS[:2], 0),
                slot(ORDERS[2:], 0),
            ]
        )
    with jax.named_scope("attend"):
        out = attention(slots, counts, query_own, query_sib, grad_own, grad_sib, gathered)
        ctx_own, gq_own, pair_sib = out[:3]
        low, mid, high = out[3::3], out[4::3], out[5::3]
    with jax.named_scope("grad_queries"):
        pair = swap(pair_sib)
        grad_rows = joined(gq_own, pair[1]).reshape(rows, head_cols)
        grad_rows, high, weight_own = lax.optimization_barrier((grad_rows, high, weight_own))
        weight_other = swap(weight_own)
        every_grad = lax.all_gather(grad_rows, "grp", axis=0, tiled=False)
    with jax.named_scope("return"):
        first = send(high, 3)
        terms, terms_sib = weight_terms(core_at, grad_rows, hidden_rows)
        context = joined(ctx_own, pair[0])
        first, terms, terms_sib, context = lax.optimization_barrier((first, terms, terms_sib, context))
        halved = combine_half("combine_high", mid, first, mid[0].shape[0])
        halved, terms, terms_sib = lax.optimization_barrier((halved, terms, terms_sib))
        second = send(halved, 2)
        terms = (terms.astype(F32) + swap(terms_sib).astype(F32)).astype(BF16)
        stays = combine_half("combine_low", low, first, 0)
        second, stays, terms = lax.optimization_barrier((second, stays, terms))
        *square, mine = combine_square(stays, second)
        square = [
            lax.ppermute(square[3 * pair + m], "chip", square_pairs(pair, m + 1))
            for pair in range(2)
            for m in range(3)
        ]
        square[0], terms = lax.optimization_barrier((square[0], terms))
        terms = lax.all_to_all(terms, "chip", split_axis=0, concat_axis=0, tiled=True)
        d_hidden = hidden_grads(core_at, every_grad, weight_own, weight_other)
        sums, sums_sib = combine_last(mine, square)
        other = swap(sums_sib)
        other, d_hidden = lax.optimization_barrier((other, d_hidden))
        d_hidden, terms = lax.optimization_barrier((d_hidden, terms))
        d_keys = joined(sums[0], other[0])
        d_values = joined(sums[1], other[1])
        d_weight = weight_sum(terms)
        d_hidden = d_hidden.reshape(spans, span_len, wide)
    return context, d_hidden, d_keys, d_values, d_weight


def solution(mesh):
    fine = Mesh(mesh.devices.reshape(mesh.devices.shape[0], CHIPS, 2), ("grp", "chip", "core"))
    placed = (
        P(NB, None, None),
        P(None, "grp"),
        P(NB, None, "grp"),
        P(NB, None, "grp"),
        P(NB, None),
        P(NB),
        P(NB, None, "grp"),
    )
    return jax.shard_map(
        per_device,
        mesh=fine,
        in_specs=placed,
        out_specs=(
            P(NB, None, "grp"),
            P(NB, None, "grp"),
            P(NB, None, "grp"),
            P(NB, None, "grp"),
            P(NB, "grp"),
        ),
        check_vma=False,
    )
```

```python
import math

import jax
import jax.numpy as jnp
from jax import lax
from jax.experimental import pallas as pl
from jax.experimental.pallas import tpu as pltpu
from jax.sharding import Mesh, PartitionSpec as P

DH = 128
SIDE = 4
CHIPS = SIDE * SIDE
NB = ("chip", "core")
F32 = jnp.float32
BF16 = jnp.bfloat16
MIB = 2**20


def chip_pairs(move):
    pairs = []
    for x in range(SIDE):
        for y in range(SIDE):
            to_x, to_y = move(x, y)
            pairs.append((x * SIDE + y, to_x * SIDE + to_y))
    return pairs


LINKS = (
    chip_pairs(lambda x, y: (x ^ 1, y)),
    chip_pairs(lambda x, y: (x, y ^ 1)),
    chip_pairs(lambda x, y: (x ^ 3, y)),
    chip_pairs(lambda x, y: (x, y ^ 3)),
)


def cube_bits(chip):
    x, y = chip // SIDE, chip % SIDE
    return ((x ^ (x >> 1)) & 1, (y ^ (y >> 1)) & 1, x >> 1, y >> 1)


ORDERS = ((0, 1, 3, 2), (0, 1, 2, 3), (2, 3, 1, 0), (2, 3, 0, 1))


def cube_place(mine, chip, order):
    here, there = cube_bits(mine), cube_bits(chip)
    across = [a ^ b for a, b in zip(here, there)]
    return sum(across[d] << k for k, d in enumerate(order))


def square_pairs(pair, bits):
    moves = [dict(LINKS[d]) for k, d in enumerate(ORDERS[2 * pair][:2]) if bits >> k & 1]
    pairs = []
    for start in range(CHIPS):
        to = start
        for move in moves:
            to = move[to]
        pairs.append((start, to))
    return pairs


def swap(value):
    return lax.ppermute(value, "core", [(0, 1), (1, 0)])


def send(streams, k):
    return [lax.ppermute(h, "chip", LINKS[ORDERS[s][k]]) for s, h in enumerate(streams)]


def in_hbm(array):
    return pltpu.with_memory_space_constraint(array, pltpu.HBM)


def add_up(block, *refs):
    total = refs[0][block].astype(F32)
    for ref in refs[1:]:
        total = total + ref[block].astype(F32)
    return total


def half_body(kept, came, out, held, sem, offset):
    size = held.shape[1]
    loads = [pltpu.make_async_copy(kept[s], held.at[s], sem.at[s]) for s in range(4)]
    for copy in loads:
        copy.start()
    for s in range(4):
        loads[s].wait()

        def step(i, carry):
            total = held[s, i].astype(F32) + came[s][offset + i].astype(F32)
            out[s][i] = total.astype(BF16)
            return carry

        lax.fori_loop(0, size, step, 0, unroll=4)


def in_vmem(body, name, out_shape, *operands):
    vmem = pl.BlockSpec(memory_space=pltpu.VMEM)
    return pl.pallas_call(
        body,
        out_shape=out_shape,
        in_specs=[vmem] * len(operands),
        out_specs=[vmem] * len(out_shape),
        compiler_params=pltpu.CompilerParams(vmem_limit_bytes=6 * MIB),
        name=name,
    )(*operands)


def combine_half(name, kept, came, offset):
    def body(*refs):
        half_body(refs[:4], refs[4:8], refs[8:12], *refs[12:], offset)

    vmem = pl.BlockSpec(memory_space=pltpu.VMEM)
    return pl.pallas_call(
        body,
        out_shape=[jax.ShapeDtypeStruct(kept[0].shape, BF16)] * 4,
        in_specs=[pl.BlockSpec(memory_space=pl.ANY)] * 4 + [vmem] * 4,
        out_specs=[vmem] * 4,
        scratch_shapes=[pltpu.VMEM((4, *kept[0].shape), BF16), pltpu.SemaphoreType.DMA((4,))],
        compiler_params=pltpu.CompilerParams(vmem_limit_bytes=6 * MIB),
        name=name,
    )(*[in_hbm(k) for k in kept], *came)


def square_body(*refs):
    cut = refs[0].shape[0] // 4
    mine = refs[14]

    def step(i, carry):
        for s in range(4):
            for m in range(3):
                total = add_up((m + 1) * cut + i, refs[s], refs[4 + s])
                refs[8 + s // 2 * 3 + m][s % 2, i] = total.astype(BF16)
            mine[s, i] = add_up(i, refs[s], refs[4 + s])
        return carry

    lax.fori_loop(0, cut, step, 0)


def combine_square(kept, came):
    size, block_len, width = kept[0].shape
    shape = jax.ShapeDtypeStruct((2, size // 4, block_len, width), BF16)
    mine = jax.ShapeDtypeStruct((4, size // 4, block_len, width), F32)
    return in_vmem(square_body, "combine_square", [shape] * 6 + [mine], *kept, *came)


def last_body(mine_in, *refs):
    came, (out_own, out_sib), (mine, held, sem) = refs[:6], refs[6:8], refs[8:]
    loads = [pltpu.make_async_copy(mine_in, mine, sem.at[6])]
    for n in range(6):
        loads.append(pltpu.make_async_copy(came[n], held.at[n], sem.at[n]))
    for copy in loads:
        copy.start()
    for copy in loads:
        copy.wait()

    def step(i, carry):
        for s in range(4):
            pair = s // 2
            total = mine[s, i]
            for n in range(3 * pair, 3 * pair + 3):
                total = total + held[n, s % 2, i].astype(F32)
            (out_sib if s % 2 else out_own)[pair, i] = total.astype(BF16)
        return carry

    lax.fori_loop(0, mine.shape[1], step, 0)


def combine_last(mine, square):
    part = (2, *mine.shape[1:])
    left = pl.BlockSpec(memory_space=pl.ANY)
    vmem = pl.BlockSpec(memory_space=pltpu.VMEM)
    return pl.pallas_call(
        last_body,
        out_shape=[jax.ShapeDtypeStruct(part, BF16)] * 2,
        in_specs=[left] * 7,
        out_specs=[vmem] * 2,
        scratch_shapes=[
            pltpu.VMEM(mine.shape, F32),
            pltpu.VMEM((6, *part), BF16),
            pltpu.SemaphoreType.DMA((7,)),
        ],
        compiler_params=pltpu.CompilerParams(vmem_limit_bytes=6 * MIB),
        name="combine_last",
    )(*[in_hbm(a) for a in (mine, *square)])


def square_join_body(*refs):
    cut = refs[0].shape[1]
    for s in range(4):
        for m in range(4):
            for i in range(cut):
                refs[8 + s][m * cut + i] = refs[2 * m + s // 2][s % 2, i]


def join_square(pairs, came):
    _, cut, block_len, width = pairs[0].shape
    shape = jax.ShapeDtypeStruct((4 * cut, block_len, width), BF16)
    return in_vmem(square_join_body, "join_square", [shape] * 4, *pairs, *came)


def join_body(*refs):
    size = refs[0].shape[0]

    def step(i, carry):
        for s in range(4):
            refs[8 + s][i] = refs[s][i]
            refs[8 + s][size + i] = refs[4 + s][i]
        return carry

    lax.fori_loop(0, size, step, 0, unroll=2)


def join_halves(held, came):
    shape = jax.ShapeDtypeStruct((2 * held[0].shape[0], *held[0].shape[1:]), BF16)
    return in_vmem(join_body, "join_halves", [shape] * 4, *held, *came)


def project_body(core, hid_ref, w_ref, own, other):
    scale = 1.0 / math.sqrt(DH)
    both = jnp.dot(hid_ref[...], w_ref[...], preferred_element_type=F32) * scale
    first, second = both[:, :DH].astype(BF16), both[:, DH:].astype(BF16)

    @pl.when(core[0] == 0)
    def _():
        own[...] = first
        other[...] = second

    @pl.when(core[0] != 0)
    def _():
        own[...] = second
        other[...] = first


def project(core, hidden_rows, query_weight):
    rows, model_width = hidden_rows.shape
    chunk = rows // 8
    out_spec = pl.BlockSpec((chunk, DH), lambda i, p: (i, 0))
    return pl.pallas_call(
        project_body,
        out_shape=[jax.ShapeDtypeStruct((rows, DH), BF16)] * 2,
        grid_spec=pltpu.PrefetchScalarGridSpec(
            num_scalar_prefetch=1,
            grid=(rows // chunk,),
            in_specs=[
                pl.BlockSpec((chunk, model_width), lambda i, p: (i, 0)),
                pl.BlockSpec(query_weight.shape, lambda i, p: (0, 0)),
            ],
            out_specs=[out_spec] * 2,
        ),
        compiler_params=pltpu.CompilerParams(vmem_limit_bytes=12 * MIB),
        name="project",
    )(core, in_hbm(hidden_rows), query_weight)


def weight_sum_body(terms, out):
    total = terms[0].astype(F32)
    for n in range(1, terms.shape[0]):
        total = total + terms[n].astype(F32)
    out[...] = total.T.astype(BF16)


def weight_sum(terms):
    _, head_cols, part = terms.shape
    shape = jax.ShapeDtypeStruct((part, head_cols), BF16)
    return in_vmem(weight_sum_body, "weight_sum", [shape], terms)[0]


def attention_body(
    slots, counts, q_own, q_sib, g_own, g_sib, *refs
):
    kv_in, (ctx_own, gq_own, pair_sib), outs = refs[:8], refs[8:11], refs[11:23]
    kv_all, dk_all, dv_all, in_sem, out_sem = refs[23:]
    scale = 1.0 / math.sqrt(DH)
    block_len = kv_all.shape[1]
    half = dk_all.shape[0] // 4
    loads = []
    for n, ref in enumerate(kv_in):
        part = kv_all.at[pl.ds(n * half, half)]
        loads.append(pltpu.make_async_copy(ref, part, in_sem.at[n]))
    for copy in loads:
        copy.start()
    blank = jnp.zeros(dk_all.shape[1:], BF16)

    def clear(n, carry):
        dk_all[n] = blank
        dv_all[n] = blank
        return carry

    lax.fori_loop(0, dk_all.shape[0], clear, 0, unroll=4)
    for copy in loads:
        copy.wait()
    spans = q_own.shape[0]
    rows = (((1,), (1,)), ((), ()))
    cols = (((0,), (0,)), ((), ()))

    def step(i, carry):
        batch = [(q_own, g_own, i, i), (q_sib, g_sib, i, i + spans)]
        q = [qr[n] for qr, _, n, _ in batch]
        g = [gr[n] for _, gr, n, _ in batch]
        refs = [(2 * span, 2 * span + 1) for _, _, _, span in batch]
        k = [jnp.concatenate([kv_all[slots[0, r]] for r in pair], axis=0) for pair in refs]
        v = [jnp.concatenate([kv_all[slots[1, r]] for r in pair], axis=0) for pair in refs]
        s = [lax.dot_general(a, b, rows, preferred_element_type=F32) for a, b in zip(q, k)]
        ga = [lax.dot_general(a, b, rows, preferred_element_type=F32) for a, b in zip(g, v)]
        place = lax.broadcasted_iota(jnp.int32, s[0].shape, 1)
        s = [
            jnp.where(place < counts[span] * block_len, a, -jnp.inf)
            for a, (_, _, _, span) in zip(s, batch)
        ]
        w = [jnp.exp(a - jnp.max(a, axis=1, keepdims=True)) for a in s]
        att = [a / jnp.sum(a, axis=1, keepdims=True) for a in w]
        low = [a.astype(BF16) for a in att]
        gs = [
            (a * (b - jnp.sum(a * b, axis=1, keepdims=True))).astype(BF16)
            for a, b in zip(att, ga)
        ]
        ctx = [jnp.dot(a, b, preferred_element_type=F32).astype(BF16) for a, b in zip(low, v)]
        gq = [(jnp.dot(a, b, preferred_element_type=F32) * scale).astype(BF16) for a, b in zip(gs, k)]
        dk = [lax.dot_general(a, b, cols, preferred_element_type=F32).astype(BF16) for a, b in zip(gs, q)]
        dv = [lax.dot_general(a, b, cols, preferred_element_type=F32).astype(BF16) for a, b in zip(low, g)]
        ctx_own[i] = ctx[0]
        gq_own[i] = gq[0]
        pair_sib[0, i] = ctx[1]
        pair_sib[1, i] = gq[1]
        for n, pair in enumerate(refs):
            for j, r in enumerate(pair):
                at = slots[2, r]
                part = dk[n][j * block_len : (j + 1) * block_len].astype(F32)
                dk_all[at] = (dk_all[at].astype(F32) + part).astype(BF16)
                at = slots[3, r]
                part = dv[n][j * block_len : (j + 1) * block_len].astype(F32)
                dv_all[at] = (dv_all[at].astype(F32) + part).astype(BF16)
        return carry

    lax.fori_loop(0, spans, step, 0, unroll=2)
    stores = []
    for s in range(4):
        whole = dk_all if s < 2 else dv_all
        at = s % 2 * 2 * half
        for ref in outs[3 * s : 3 * s + 3]:
            size = ref.shape[0]
            stores.append(
                pltpu.make_async_copy(whole.at[pl.ds(at, size)], ref, out_sem.at[len(stores)])
            )
            at += size
    for copy in stores:
        copy.start()
    for copy in stores:
        copy.wait()


def attention(slots, counts, q_own, q_sib, g_own, g_sib, gathered):
    spans, span_len, width = q_own.shape
    half, block_len, _ = gathered[0].shape
    small = jax.ShapeDtypeStruct((spans, span_len, width), BF16)
    pair = jax.ShapeDtypeStruct((2, spans, span_len, width), BF16)
    pieces = [half // 2, half // 2, half] * 4
    large = [pltpu.HBM((n, block_len, width), BF16) for n in pieces]
    grads = pltpu.VMEM((4 * half, block_len, width), BF16)
    smem = pl.BlockSpec(memory_space=pltpu.SMEM)
    vmem = pl.BlockSpec(memory_space=pltpu.VMEM)
    hbm = pl.BlockSpec(memory_space=pltpu.HBM)
    left = pl.BlockSpec(memory_space=pl.ANY)
    return pl.pallas_call(
        attention_body,
        out_shape=[small, small, pair] + large,
        in_specs=[smem] * 2 + [vmem] * 4 + [left] * 8,
        out_specs=[vmem] * 3 + [hbm] * 12,
        scratch_shapes=[
            pltpu.VMEM((8 * half, block_len, width), BF16),
            grads,
            grads,
            pltpu.SemaphoreType.DMA((8,)),
            pltpu.SemaphoreType.DMA((12,)),
        ],
        compiler_params=pltpu.CompilerParams(vmem_limit_bytes=20 * MIB),
        name="attention",
    )(slots, counts, q_own, q_sib, g_own, g_sib, *[in_hbm(a) for a in gathered])


def weight_body(core, gq_ref, hid_ref, own, sib, gq_t):
    step = pl.program_id(0)

    @pl.when(step == 0)
    def _():
        gq_t[...] = gq_ref[...].T

    term = jnp.dot(gq_t[...], hid_ref[...], preferred_element_type=F32).astype(BF16)
    chips, _, part = own.shape
    for n in range(chips):
        even = term[:, 2 * n * part : (2 * n + 1) * part]
        odd = term[:, (2 * n + 1) * part : (2 * n + 2) * part]

        @pl.when(core[0] == 0)
        def _():
            own[n] = even
            sib[n] = odd

        @pl.when(core[0] != 0)
        def _():
            own[n] = odd
            sib[n] = even


def weight_terms(core, grad_rows, hidden_rows):
    rows, model_width = hidden_rows.shape
    head_cols = grad_rows.shape[1]
    part = model_width // (2 * CHIPS)
    chips = 2
    wide = 2 * chips * part
    out_spec = pl.BlockSpec((chips, head_cols, part), lambda i, p: (i, 0, 0))
    return pl.pallas_call(
        weight_body,
        out_shape=[jax.ShapeDtypeStruct((CHIPS, head_cols, part), BF16)] * 2,
        grid_spec=pltpu.PrefetchScalarGridSpec(
            num_scalar_prefetch=1,
            grid=(CHIPS // chips,),
            in_specs=[
                pl.BlockSpec(grad_rows.shape, lambda i, p: (0, 0)),
                pl.BlockSpec((rows, wide), lambda i, p: (0, i)),
            ],
            out_specs=[out_spec] * 2,
            scratch_shapes=[pltpu.VMEM(grad_rows.shape[::-1], BF16)],
        ),
        compiler_params=pltpu.CompilerParams(vmem_limit_bytes=12 * MIB),
        name="weight_terms",
    )(core, grad_rows, in_hbm(hidden_rows))


def hidden_body(core, gq_ref, mine, other, out):
    wide = mine.shape[1]
    for n, w_ref in enumerate((mine, other)):
        total = None
        for g in range(gq_ref.shape[0]):
            term = lax.dot_general(
                gq_ref[g], w_ref[g], (((1,), (1,)), ((), ())), preferred_element_type=F32
            )
            term = term.astype(BF16).astype(F32)
            total = term if total is None else total + term
        at = pl.multiple_of((core[0] if n == 0 else 1 - core[0]) * wide, wide)
        out[:, pl.ds(at, wide)] = total.astype(BF16)


def hidden_grads(core, every_grad, mine, other):
    groups, rows, head_cols = every_grad.shape
    wide = 2 * mine.shape[1]
    chunk = rows // 4
    return pl.pallas_call(
        hidden_body,
        out_shape=jax.ShapeDtypeStruct((rows, wide), BF16),
        grid_spec=pltpu.PrefetchScalarGridSpec(
            num_scalar_prefetch=1,
            grid=(rows // chunk,),
            in_specs=[
                pl.BlockSpec((groups, chunk, head_cols), lambda i, p: (0, i, 0)),
                pl.BlockSpec(mine.shape, lambda i, p: (0, 0, 0)),
                pl.BlockSpec(mine.shape, lambda i, p: (0, 0, 0)),
            ],
            out_specs=pl.BlockSpec((chunk, wide), lambda i, p: (i, 0)),
        ),
        compiler_params=pltpu.CompilerParams(vmem_limit_bytes=16 * MIB),
        name="hidden_grads",
    )(core, in_hbm(every_grad), mine, other)


def per_device(hidden, query_weight, keys, values, neighbour_ids, neighbour_counts, d_context):
    spans, span_len, model_width = hidden.shape
    blocks, block_len, head_cols = keys.shape
    groups = lax.axis_size("grp")
    chip = lax.axis_index("chip")
    core = lax.axis_index("core")
    core_at = core.reshape(1)
    rows = spans * span_len
    refs = neighbour_ids.size

    def both(array):
        first, second = array[..., :DH], array[..., DH:]
        return jnp.where(core == 0, first, second), jnp.where(core == 0, second, first)

    def joined(own, other):
        return jnp.where(
            core == 0,
            jnp.concatenate([own, other], axis=-1),
            jnp.concatenate([other, own], axis=-1),
        )

    with jax.named_scope("gather"):
        own, other = both(jnp.stack([keys, values]))
        came = swap(other)
        pairs = lax.optimization_barrier(
            [jnp.stack([own[0], came[0]]), jnp.stack([own[1], came[1]])]
        )

        def across(pieces, k):
            return [lax.ppermute(p, "chip", LINKS[ORDERS[s][k]]) for s, p in enumerate(pieces)]

        came = [
            lax.ppermute(pairs[pair], "chip", square_pairs(pair, m))
            for m in (1, 2, 3)
            for pair in range(2)
        ]
        held = join_square(pairs, came)
        held = join_halves(held, across(held, 2))
        last = across(held, 3)
    with jax.named_scope("queries"):
        hidden_rows = hidden.reshape(rows, model_width)
        query_own, query_other = project(core_at, hidden_rows, query_weight)
        query_own, query_other, leaving = lax.optimization_barrier(
            (query_own, query_other, query_weight)
        )
        last, query_own, query_other = lax.optimization_barrier((last, query_own, query_other))
        gathered = [part for parts in zip(held, last) for part in parts]
        query_own = query_own.reshape(spans, span_len, DH)
        query_sib = swap(query_other.reshape(spans, span_len, DH))
    with jax.named_scope("weight_rows"):
        wide = model_width // groups
        asked = leaving.reshape(groups, 2, wide // 2, head_cols)
        asked = jnp.where(core == 0, asked[:, 0], asked[:, 1])
        weight_own = lax.all_to_all(asked, "grp", split_axis=0, concat_axis=0, tiled=True)
    with jax.named_scope("more"):
        grad_own, grad_other = both(d_context)
        grad_sib = swap(grad_other)
    with jax.named_scope("slots"):
        table = jnp.concatenate([neighbour_ids.reshape(-1), neighbour_counts])
        table_sib = swap(table)
        ids = jnp.concatenate([table[:refs], table_sib[:refs]])
        counts = jnp.concatenate([table[refs:], table_sib[refs:]])
        owner, local = ids // blocks, ids % blocks
        far = jnp.where(owner % 2 == core, 0, 1)
        host = owner // 2

        def slot(orders, first):
            near_place = cube_place(chip, host, orders[0])
            far_place = CHIPS + cube_place(chip, host, orders[1])
            return (first + jnp.where(far == 0, near_place, far_place)) * blocks + local

        slots = jnp.stack(
            [
                slot(ORDERS[:2], 0),
                slot(ORDERS[2:], 2 * CHIPS),
                slot(ORDERS[:2], 0),
                slot(ORDERS[2:], 0),
            ]
        )
    with jax.named_scope("attend"):
        out = attention(slots, counts, query_own, query_sib, grad_own, grad_sib, gathered)
        ctx_own, gq_own, pair_sib = out[:3]
        low, mid, high = out[3::3], out[4::3], out[5::3]
    with jax.named_scope("grad_queries"):
        pair = swap(pair_sib)
        grad_rows = joined(gq_own, pair[1]).reshape(rows, head_cols)
        grad_rows, high, weight_own = lax.optimization_barrier((grad_rows, high, weight_own))
        weight_other = swap(weight_own)
        every_grad = lax.all_gather(grad_rows, "grp", axis=0, tiled=False)
    with jax.named_scope("return"):
        first = send(high, 3)
        terms, terms_sib = weight_terms(core_at, grad_rows, hidden_rows)
        context = joined(ctx_own, pair[0])
        first, terms, terms_sib, context = lax.optimization_barrier((first, terms, terms_sib, context))
        halved = combine_half("combine_high", mid, first, mid[0].shape[0])
        halved, terms, terms_sib = lax.optimization_barrier((halved, terms, terms_sib))
        second = send(halved, 2)
        terms = (terms.astype(F32) + swap(terms_sib).astype(F32)).astype(BF16)
        stays = combine_half("combine_low", low, first, 0)
        second, stays, terms = lax.optimization_barrier((second, stays, terms))
        *square, mine = combine_square(stays, second)
        square = [
            lax.ppermute(square[3 * pair + m], "chip", square_pairs(pair, m + 1))
            for pair in range(2)
            for m in range(3)
        ]
        square, mine, terms = lax.optimization_barrier((square, mine, terms))
        terms = lax.all_to_all(terms, "chip", split_axis=0, concat_axis=0, tiled=True)
        d_hidden = hidden_grads(core_at, every_grad, weight_own, weight_other)
        sums, sums_sib = combine_last(mine, square)
        other = swap(sums_sib)
        other, d_hidden = lax.optimization_barrier((other, d_hidden))
        d_hidden, terms = lax.optimization_barrier((d_hidden, terms))
        d_keys = joined(sums[0], other[0])
        d_values = joined(sums[1], other[1])
        d_weight = weight_sum(terms)
        d_hidden = d_hidden.reshape(spans, span_len, wide)
    return context, d_hidden, d_keys, d_values, d_weight


def solution(mesh):
    fine = Mesh(mesh.devices.reshape(mesh.devices.shape[0], CHIPS, 2), ("grp", "chip", "core"))
    placed = (
        P(NB, None, None),
        P(None, "grp"),
        P(NB, None, "grp"),
        P(NB, None, "grp"),
        P(NB, None),
        P(NB),
        P(NB, None, "grp"),
    )
    return jax.shard_map(
        per_device,
        mesh=fine,
        in_specs=placed,
        out_specs=(
            P(NB, None, "grp"),
            P(NB, None, "grp"),
            P(NB, None, "grp"),
            P(NB, None, "grp"),
            P(NB, "grp"),
        ),
        check_vma=False,
    )
```

```python
import math

import jax
import jax.numpy as jnp
from jax import lax
from jax.experimental import pallas as pl
from jax.experimental.pallas import tpu as pltpu
from jax.sharding import Mesh, PartitionSpec as P

DH = 128
SIDE = 4
CHIPS = SIDE * SIDE
NB = ("chip", "core")
F32 = jnp.float32
BF16 = jnp.bfloat16
MIB = 2**20
PARTS = 4


def chip_pairs(move):
    pairs = []
    for x in range(SIDE):
        for y in range(SIDE):
            to_x, to_y = move(x, y)
            pairs.append((x * SIDE + y, to_x * SIDE + to_y))
    return pairs


LINKS = (
    chip_pairs(lambda x, y: (x ^ 1, y)),
    chip_pairs(lambda x, y: (x, y ^ 1)),
    chip_pairs(lambda x, y: (x ^ 3, y)),
    chip_pairs(lambda x, y: (x, y ^ 3)),
)


def cube_bits(chip):
    x, y = chip // SIDE, chip % SIDE
    return ((x ^ (x >> 1)) & 1, (y ^ (y >> 1)) & 1, x >> 1, y >> 1)


ORDERS = ((0, 1, 3, 2), (0, 1, 2, 3), (2, 3, 1, 0), (2, 3, 0, 1))


def cube_place(mine, chip, order):
    here, there = cube_bits(mine), cube_bits(chip)
    across = [a ^ b for a, b in zip(here, there)]
    return sum(across[d] << k for k, d in enumerate(order))


def square_pairs(pair, bits):
    moves = [dict(LINKS[d]) for k, d in enumerate(ORDERS[2 * pair][:2]) if bits >> k & 1]
    pairs = []
    for start in range(CHIPS):
        to = start
        for move in moves:
            to = move[to]
        pairs.append((start, to))
    return pairs


def swap(value):
    return lax.ppermute(value, "core", [(0, 1), (1, 0)])


def send(streams, k):
    return [lax.ppermute(h, "chip", LINKS[ORDERS[s][k]]) for s, h in enumerate(streams)]


def in_hbm(array):
    return pltpu.with_memory_space_constraint(array, pltpu.HBM)


def add_up(block, *refs):
    total = refs[0][block].astype(F32)
    for ref in refs[1:]:
        total = total + ref[block].astype(F32)
    return total


def half_body(kept, came, out, held, sem, offset):
    size = held.shape[1]
    loads = [pltpu.make_async_copy(kept[s], held.at[s], sem.at[s]) for s in range(4)]
    for copy in loads:
        copy.start()
    for s in range(4):
        loads[s].wait()

        def step(i, carry):
            total = held[s, i].astype(F32) + came[s][offset + i].astype(F32)
            out[s][i] = total.astype(BF16)
            return carry

        lax.fori_loop(0, size, step, 0, unroll=4)


def in_vmem(body, name, out_shape, *operands):
    vmem = pl.BlockSpec(memory_space=pltpu.VMEM)
    return pl.pallas_call(
        body,
        out_shape=out_shape,
        in_specs=[vmem] * len(operands),
        out_specs=[vmem] * len(out_shape),
        compiler_params=pltpu.CompilerParams(vmem_limit_bytes=6 * MIB),
        name=name,
    )(*operands)


def combine_half(name, kept, came, offset):
    def body(*refs):
        half_body(refs[:4], refs[4:8], refs[8:12], *refs[12:], offset)

    vmem = pl.BlockSpec(memory_space=pltpu.VMEM)
    return pl.pallas_call(
        body,
        out_shape=[jax.ShapeDtypeStruct(kept[0].shape, BF16)] * 4,
        in_specs=[pl.BlockSpec(memory_space=pl.ANY)] * 4 + [vmem] * 4,
        out_specs=[vmem] * 4,
        scratch_shapes=[pltpu.VMEM((4, *kept[0].shape), BF16), pltpu.SemaphoreType.DMA((4,))],
        compiler_params=pltpu.CompilerParams(vmem_limit_bytes=6 * MIB),
        name=name,
    )(*[in_hbm(k) for k in kept], *came)


def square_body(*refs):
    cut = refs[0].shape[0] // 4
    mine = refs[14]

    def step(i, carry):
        for s in range(4):
            for m in range(3):
                total = add_up((m + 1) * cut + i, refs[s], refs[4 + s])
                refs[8 + s // 2 * 3 + m][s % 2, i] = total.astype(BF16)
            mine[s, i] = add_up(i, refs[s], refs[4 + s])
        return carry

    lax.fori_loop(0, cut, step, 0)


def combine_square(kept, came):
    size, block_len, width = kept[0].shape
    shape = jax.ShapeDtypeStruct((2, size // 4, block_len, width), BF16)
    mine = jax.ShapeDtypeStruct((4, size // 4, block_len, width), F32)
    return in_vmem(square_body, "combine_square", [shape] * 6 + [mine], *kept, *came)


def last_body(mine_in, *refs):
    came, (out_own, out_sib), (mine, held, sem) = refs[:6], refs[6:8], refs[8:]
    loads = [pltpu.make_async_copy(mine_in, mine, sem.at[6])]
    for n in range(6):
        loads.append(pltpu.make_async_copy(came[n], held.at[n], sem.at[n]))
    for copy in loads:
        copy.start()
    for copy in loads:
        copy.wait()

    def step(i, carry):
        for s in range(4):
            pair = s // 2
            total = mine[s, i]
            for n in range(3 * pair, 3 * pair + 3):
                total = total + held[n, s % 2, i].astype(F32)
            (out_sib if s % 2 else out_own)[pair, i] = total.astype(BF16)
        return carry

    lax.fori_loop(0, mine.shape[1], step, 0)


def combine_last(mine, square):
    part = (2, *mine.shape[1:])
    left = pl.BlockSpec(memory_space=pl.ANY)
    vmem = pl.BlockSpec(memory_space=pltpu.VMEM)
    return pl.pallas_call(
        last_body,
        out_shape=[jax.ShapeDtypeStruct(part, BF16)] * 2,
        in_specs=[left] * 7,
        out_specs=[vmem] * 2,
        scratch_shapes=[
            pltpu.VMEM(mine.shape, F32),
            pltpu.VMEM((6, *part), BF16),
            pltpu.SemaphoreType.DMA((7,)),
        ],
        compiler_params=pltpu.CompilerParams(vmem_limit_bytes=6 * MIB),
        name="combine_last",
    )(*[in_hbm(a) for a in (mine, *square)])


def square_join_body(*refs):
    cut = refs[0].shape[1]
    for s in range(4):
        for m in range(4):
            for i in range(cut):
                refs[8 + s][m * cut + i] = refs[2 * m + s // 2][s % 2, i]


def join_square(pairs, came):
    _, cut, block_len, width = pairs[0].shape
    shape = jax.ShapeDtypeStruct((4 * cut, block_len, width), BF16)
    return in_vmem(square_join_body, "join_square", [shape] * 4, *pairs, *came)


def join_body(*refs):
    size = refs[0].shape[0]

    def step(i, carry):
        for s in range(4):
            refs[8 + s][i] = refs[s][i]
            refs[8 + s][size + i] = refs[4 + s][i]
        return carry

    lax.fori_loop(0, size, step, 0, unroll=2)


def join_halves(held, came):
    shape = jax.ShapeDtypeStruct((2 * held[0].shape[0], *held[0].shape[1:]), BF16)
    return in_vmem(join_body, "join_halves", [shape] * 4, *held, *came)


def project_body(core, hid_ref, w_ref, own, other):
    scale = 1.0 / math.sqrt(DH)
    both = jnp.dot(hid_ref[...], w_ref[...], preferred_element_type=F32) * scale
    first, second = both[:, :DH].astype(BF16), both[:, DH:].astype(BF16)

    @pl.when(core[0] == 0)
    def _():
        own[...] = first
        other[...] = second

    @pl.when(core[0] != 0)
    def _():
        own[...] = second
        other[...] = first


def project(core, hidden_rows, query_weight):
    rows, model_width = hidden_rows.shape
    chunk = rows // 8
    out_spec = pl.BlockSpec((chunk, DH), lambda i, p: (i, 0))
    return pl.pallas_call(
        project_body,
        out_shape=[jax.ShapeDtypeStruct((rows, DH), BF16)] * 2,
        grid_spec=pltpu.PrefetchScalarGridSpec(
            num_scalar_prefetch=1,
            grid=(rows // chunk,),
            in_specs=[
                pl.BlockSpec((chunk, model_width), lambda i, p: (i, 0)),
                pl.BlockSpec(query_weight.shape, lambda i, p: (0, 0)),
            ],
            out_specs=[out_spec] * 2,
        ),
        compiler_params=pltpu.CompilerParams(vmem_limit_bytes=12 * MIB),
        name="project",
    )(core, in_hbm(hidden_rows), query_weight)


def weight_sum_body(terms, out):
    total = terms[0].astype(F32)
    for n in range(1, terms.shape[0]):
        total = total + terms[n].astype(F32)
    out[...] = total.T.astype(BF16)


def weight_sum(terms):
    _, head_cols, part = terms.shape
    shape = jax.ShapeDtypeStruct((part, head_cols), BF16)
    return in_vmem(weight_sum_body, "weight_sum", [shape], terms)[0]


def attention_body(
    slots, counts, q_own, q_sib, g_own, g_sib, *refs
):
    kv_in, (ctx_own, gq_own, pair_sib), outs = refs[:8], refs[8:11], refs[11:23]
    kv_all, dk_all, dv_all, in_sem, out_sem = refs[23:]
    scale = 1.0 / math.sqrt(DH)
    block_len = kv_all.shape[1]
    half = dk_all.shape[0] // 4
    loads = []
    for n, ref in enumerate(kv_in):
        part = kv_all.at[pl.ds(n * half, half)]
        loads.append(pltpu.make_async_copy(ref, part, in_sem.at[n]))
    for copy in loads:
        copy.start()
    blank = jnp.zeros(dk_all.shape[1:], BF16)

    def clear(n, carry):
        dk_all[n] = blank
        dv_all[n] = blank
        return carry

    lax.fori_loop(0, dk_all.shape[0], clear, 0, unroll=4)
    for copy in loads:
        copy.wait()
    spans = q_own.shape[0]
    rows = (((1,), (1,)), ((), ()))
    cols = (((0,), (0,)), ((), ()))

    def step(i, carry):
        batch = []
        for part in range(PARTS):
            at = i + part * (spans // PARTS)
            batch += [(q_own, g_own, at, at), (q_sib, g_sib, at, at + spans)]
        q = [qr[n] for qr, _, n, _ in batch]
        g = [gr[n] for _, gr, n, _ in batch]
        refs = [(2 * span, 2 * span + 1) for _, _, _, span in batch]
        k = [jnp.concatenate([kv_all[slots[0, r]] for r in pair], axis=0) for pair in refs]
        v = [jnp.concatenate([kv_all[slots[1, r]] for r in pair], axis=0) for pair in refs]
        s = [lax.dot_general(a, b, rows, preferred_element_type=F32) for a, b in zip(q, k)]
        ga = [lax.dot_general(a, b, rows, preferred_element_type=F32) for a, b in zip(g, v)]
        place = lax.broadcasted_iota(jnp.int32, s[0].shape, 1)
        s = [
            jnp.where(place < counts[span] * block_len, a, -jnp.inf)
            for a, (_, _, _, span) in zip(s, batch)
        ]
        w = [jnp.exp(a - jnp.max(a, axis=1, keepdims=True)) for a in s]
        att = [a / jnp.sum(a, axis=1, keepdims=True) for a in w]
        low = [a.astype(BF16) for a in att]
        gs = [
            (a * (b - jnp.sum(a * b, axis=1, keepdims=True))).astype(BF16)
            for a, b in zip(att, ga)
        ]
        ctx = [jnp.dot(a, b, preferred_element_type=F32).astype(BF16) for a, b in zip(low, v)]
        gq = [(jnp.dot(a, b, preferred_element_type=F32) * scale).astype(BF16) for a, b in zip(gs, k)]
        dk = [lax.dot_general(a, b, cols, preferred_element_type=F32).astype(BF16) for a, b in zip(gs, q)]
        dv = [lax.dot_general(a, b, cols, preferred_element_type=F32).astype(BF16) for a, b in zip(low, g)]
        for n in range(0, len(batch), 2):
            at = batch[n][2]
            ctx_own[at] = ctx[n]
            gq_own[at] = gq[n]
            pair_sib[0, at] = ctx[n + 1]
            pair_sib[1, at] = gq[n + 1]
        for n, pair in enumerate(refs):
            for j, r in enumerate(pair):
                at = slots[2, r]
                part = dk[n][j * block_len : (j + 1) * block_len].astype(F32)
                dk_all[at] = (dk_all[at].astype(F32) + part).astype(BF16)
                at = slots[3, r]
                part = dv[n][j * block_len : (j + 1) * block_len].astype(F32)
                dv_all[at] = (dv_all[at].astype(F32) + part).astype(BF16)
        return carry

    lax.fori_loop(0, spans // PARTS, step, 0)
    stores = []
    for s in range(4):
        whole = dk_all if s < 2 else dv_all
        at = s % 2 * 2 * half
        for ref in outs[3 * s : 3 * s + 3]:
            size = ref.shape[0]
            stores.append(
                pltpu.make_async_copy(whole.at[pl.ds(at, size)], ref, out_sem.at[len(stores)])
            )
            at += size
    for copy in stores:
        copy.start()
    for copy in stores:
        copy.wait()


def attention(slots, counts, q_own, q_sib, g_own, g_sib, gathered):
    spans, span_len, width = q_own.shape
    half, block_len, _ = gathered[0].shape
    small = jax.ShapeDtypeStruct((spans, span_len, width), BF16)
    pair = jax.ShapeDtypeStruct((2, spans, span_len, width), BF16)
    pieces = [half // 2, half // 2, half] * 4
    large = [pltpu.HBM((n, block_len, width), BF16) for n in pieces]
    grads = pltpu.VMEM((4 * half, block_len, width), BF16)
    smem = pl.BlockSpec(memory_space=pltpu.SMEM)
    vmem = pl.BlockSpec(memory_space=pltpu.VMEM)
    hbm = pl.BlockSpec(memory_space=pltpu.HBM)
    left = pl.BlockSpec(memory_space=pl.ANY)
    return pl.pallas_call(
        attention_body,
        out_shape=[small, small, pair] + large,
        in_specs=[smem] * 2 + [vmem] * 4 + [left] * 8,
        out_specs=[vmem] * 3 + [hbm] * 12,
        scratch_shapes=[
            pltpu.VMEM((8 * half, block_len, width), BF16),
            grads,
            grads,
            pltpu.SemaphoreType.DMA((8,)),
            pltpu.SemaphoreType.DMA((12,)),
        ],
        compiler_params=pltpu.CompilerParams(vmem_limit_bytes=20 * MIB),
        name="attention",
    )(slots, counts, q_own, q_sib, g_own, g_sib, *[in_hbm(a) for a in gathered])


def weight_body(core, gq_ref, hid_ref, own, sib, gq_t):
    step = pl.program_id(0)

    @pl.when(step == 0)
    def _():
        gq_t[...] = gq_ref[...].T

    term = jnp.dot(gq_t[...], hid_ref[...], preferred_element_type=F32).astype(BF16)
    chips, _, part = own.shape
    for n in range(chips):
        even = term[:, 2 * n * part : (2 * n + 1) * part]
        odd = term[:, (2 * n + 1) * part : (2 * n + 2) * part]

        @pl.when(core[0] == 0)
        def _():
            own[n] = even
            sib[n] = odd

        @pl.when(core[0] != 0)
        def _():
            own[n] = odd
            sib[n] = even


def weight_terms(core, grad_rows, hidden_rows):
    rows, model_width = hidden_rows.shape
    head_cols = grad_rows.shape[1]
    part = model_width // (2 * CHIPS)
    chips = 2
    wide = 2 * chips * part
    out_spec = pl.BlockSpec((chips, head_cols, part), lambda i, p: (i, 0, 0))
    return pl.pallas_call(
        weight_body,
        out_shape=[jax.ShapeDtypeStruct((CHIPS, head_cols, part), BF16)] * 2,
        grid_spec=pltpu.PrefetchScalarGridSpec(
            num_scalar_prefetch=1,
            grid=(CHIPS // chips,),
            in_specs=[
                pl.BlockSpec(grad_rows.shape, lambda i, p: (0, 0)),
                pl.BlockSpec((rows, wide), lambda i, p: (0, i)),
            ],
            out_specs=[out_spec] * 2,
            scratch_shapes=[pltpu.VMEM(grad_rows.shape[::-1], BF16)],
        ),
        compiler_params=pltpu.CompilerParams(vmem_limit_bytes=12 * MIB),
        name="weight_terms",
    )(core, grad_rows, in_hbm(hidden_rows))


def hidden_body(core, gq_ref, mine, other, out):
    wide = mine.shape[1]
    for n, w_ref in enumerate((mine, other)):
        total = None
        for g in range(gq_ref.shape[0]):
            term = lax.dot_general(
                gq_ref[g], w_ref[g], (((1,), (1,)), ((), ())), preferred_element_type=F32
            )
            term = term.astype(BF16).astype(F32)
            total = term if total is None else total + term
        at = pl.multiple_of((core[0] if n == 0 else 1 - core[0]) * wide, wide)
        out[:, pl.ds(at, wide)] = total.astype(BF16)


def hidden_grads(core, every_grad, mine, other):
    groups, rows, head_cols = every_grad.shape
    wide = 2 * mine.shape[1]
    chunk = rows // 4
    return pl.pallas_call(
        hidden_body,
        out_shape=jax.ShapeDtypeStruct((rows, wide), BF16),
        grid_spec=pltpu.PrefetchScalarGridSpec(
            num_scalar_prefetch=1,
            grid=(rows // chunk,),
            in_specs=[
                pl.BlockSpec((groups, chunk, head_cols), lambda i, p: (0, i, 0)),
                pl.BlockSpec(mine.shape, lambda i, p: (0, 0, 0)),
                pl.BlockSpec(mine.shape, lambda i, p: (0, 0, 0)),
            ],
            out_specs=pl.BlockSpec((chunk, wide), lambda i, p: (i, 0)),
        ),
        compiler_params=pltpu.CompilerParams(vmem_limit_bytes=16 * MIB),
        name="hidden_grads",
    )(core, in_hbm(every_grad), mine, other)


def per_device(hidden, query_weight, keys, values, neighbour_ids, neighbour_counts, d_context):
    spans, span_len, model_width = hidden.shape
    blocks, block_len, head_cols = keys.shape
    groups = lax.axis_size("grp")
    chip = lax.axis_index("chip")
    core = lax.axis_index("core")
    core_at = core.reshape(1)
    rows = spans * span_len
    refs = neighbour_ids.size

    def both(array):
        first, second = array[..., :DH], array[..., DH:]
        return jnp.where(core == 0, first, second), jnp.where(core == 0, second, first)

    def joined(own, other):
        return jnp.where(
            core == 0,
            jnp.concatenate([own, other], axis=-1),
            jnp.concatenate([other, own], axis=-1),
        )

    with jax.named_scope("gather"):
        own, other = both(jnp.stack([keys, values]))
        came = swap(other)
        pairs = lax.optimization_barrier(
            [jnp.stack([own[0], came[0]]), jnp.stack([own[1], came[1]])]
        )

        def across(pieces, k):
            return [lax.ppermute(p, "chip", LINKS[ORDERS[s][k]]) for s, p in enumerate(pieces)]

        came = [
            lax.ppermute(pairs[pair], "chip", square_pairs(pair, m))
            for m in (1, 2, 3)
            for pair in range(2)
        ]
        held = join_square(pairs, came)
        held = join_halves(held, across(held, 2))
        last = across(held, 3)
    with jax.named_scope("queries"):
        hidden_rows = hidden.reshape(rows, model_width)
        query_own, query_other = project(core_at, hidden_rows, query_weight)
        query_own, query_other, leaving = lax.optimization_barrier(
            (query_own, query_other, query_weight)
        )
        last, query_own, query_other = lax.optimization_barrier((last, query_own, query_other))
        gathered = [part for parts in zip(held, last) for part in parts]
        query_own = query_own.reshape(spans, span_len, DH)
        query_sib = swap(query_other.reshape(spans, span_len, DH))
    with jax.named_scope("weight_rows"):
        wide = model_width // groups
        asked = leaving.reshape(groups, 2, wide // 2, head_cols)
        asked = jnp.where(core == 0, asked[:, 0], asked[:, 1])
        weight_own = lax.all_to_all(asked, "grp", split_axis=0, concat_axis=0, tiled=True)
    with jax.named_scope("more"):
        grad_own, grad_other = both(d_context)
        grad_sib = swap(grad_other)
    with jax.named_scope("slots"):
        table = jnp.concatenate([neighbour_ids.reshape(-1), neighbour_counts])
        table_sib = swap(table)
        ids = jnp.concatenate([table[:refs], table_sib[:refs]])
        counts = jnp.concatenate([table[refs:], table_sib[refs:]])
        owner, local = ids // blocks, ids % blocks
        far = jnp.where(owner % 2 == core, 0, 1)
        host = owner // 2

        def slot(orders, first):
            near_place = cube_place(chip, host, orders[0])
            far_place = CHIPS + cube_place(chip, host, orders[1])
            return (first + jnp.where(far == 0, near_place, far_place)) * blocks + local

        slots = jnp.stack(
            [
                slot(ORDERS[:2], 0),
                slot(ORDERS[2:], 2 * CHIPS),
                slot(ORDERS[:2], 0),
                slot(ORDERS[2:], 0),
            ]
        )
    with jax.named_scope("attend"):
        out = attention(slots, counts, query_own, query_sib, grad_own, grad_sib, gathered)
        ctx_own, gq_own, pair_sib = out[:3]
        low, mid, high = out[3::3], out[4::3], out[5::3]
    with jax.named_scope("grad_queries"):
        pair = swap(pair_sib)
        grad_rows = joined(gq_own, pair[1]).reshape(rows, head_cols)
        grad_rows, high, weight_own = lax.optimization_barrier((grad_rows, high, weight_own))
        weight_other = swap(weight_own)
        every_grad = lax.all_gather(grad_rows, "grp", axis=0, tiled=False)
    with jax.named_scope("return"):
        first = send(high, 3)
        terms, terms_sib = weight_terms(core_at, grad_rows, hidden_rows)
        context = joined(ctx_own, pair[0])
        first, terms, terms_sib, context = lax.optimization_barrier((first, terms, terms_sib, context))
        halved = combine_half("combine_high", mid, first, mid[0].shape[0])
        halved, terms, terms_sib = lax.optimization_barrier((halved, terms, terms_sib))
        second = send(halved, 2)
        terms = (terms.astype(F32) + swap(terms_sib).astype(F32)).astype(BF16)
        stays = combine_half("combine_low", low, first, 0)
        second, stays, terms = lax.optimization_barrier((second, stays, terms))
        *square, mine = combine_square(stays, second)
        square = [
            lax.ppermute(square[3 * pair + m], "chip", square_pairs(pair, m + 1))
            for pair in range(2)
            for m in range(3)
        ]
        square, mine, terms = lax.optimization_barrier((square, mine, terms))
        terms = lax.all_to_all(terms, "chip", split_axis=0, concat_axis=0, tiled=True)
        d_hidden = hidden_grads(core_at, every_grad, weight_own, weight_other)
        sums, sums_sib = combine_last(mine, square)
        other = swap(sums_sib)
        other, d_hidden = lax.optimization_barrier((other, d_hidden))
        d_hidden, terms = lax.optimization_barrier((d_hidden, terms))
        d_keys = joined(sums[0], other[0])
        d_values = joined(sums[1], other[1])
        d_weight = weight_sum(terms)
        d_hidden = d_hidden.reshape(spans, span_len, wide)
    return context, d_hidden, d_keys, d_values, d_weight


def solution(mesh):
    fine = Mesh(mesh.devices.reshape(mesh.devices.shape[0], CHIPS, 2), ("grp", "chip", "core"))
    placed = (
        P(NB, None, None),
        P(None, "grp"),
        P(NB, None, "grp"),
        P(NB, None, "grp"),
        P(NB, None),
        P(NB),
        P(NB, None, "grp"),
    )
    return jax.shard_map(
        per_device,
        mesh=fine,
        in_specs=placed,
        out_specs=(
            P(NB, None, "grp"),
            P(NB, None, "grp"),
            P(NB, None, "grp"),
            P(NB, None, "grp"),
            P(NB, "grp"),
        ),
        check_vma=False,
    )
```

```python
import math

import jax
import jax.numpy as jnp
from jax import lax
from jax.experimental import pallas as pl
from jax.experimental.pallas import tpu as pltpu
from jax.sharding import Mesh, PartitionSpec as P

DH = 128
SIDE = 4
CHIPS = SIDE * SIDE
NB = ("chip", "core")
F32 = jnp.float32
BF16 = jnp.bfloat16
MIB = 2**20
PARTS = 8


def chip_pairs(move):
    pairs = []
    for x in range(SIDE):
        for y in range(SIDE):
            to_x, to_y = move(x, y)
            pairs.append((x * SIDE + y, to_x * SIDE + to_y))
    return pairs


LINKS = (
    chip_pairs(lambda x, y: (x ^ 1, y)),
    chip_pairs(lambda x, y: (x, y ^ 1)),
    chip_pairs(lambda x, y: (x ^ 3, y)),
    chip_pairs(lambda x, y: (x, y ^ 3)),
)


def cube_bits(chip):
    x, y = chip // SIDE, chip % SIDE
    return ((x ^ (x >> 1)) & 1, (y ^ (y >> 1)) & 1, x >> 1, y >> 1)


ORDERS = ((0, 1, 3, 2), (0, 1, 2, 3), (2, 3, 1, 0), (2, 3, 0, 1))


def cube_place(mine, chip, order):
    here, there = cube_bits(mine), cube_bits(chip)
    across = [a ^ b for a, b in zip(here, there)]
    return sum(across[d] << k for k, d in enumerate(order))


def square_pairs(pair, bits):
    moves = [dict(LINKS[d]) for k, d in enumerate(ORDERS[2 * pair][:2]) if bits >> k & 1]
    pairs = []
    for start in range(CHIPS):
        to = start
        for move in moves:
            to = move[to]
        pairs.append((start, to))
    return pairs


def swap(value):
    return lax.ppermute(value, "core", [(0, 1), (1, 0)])


def send(streams, k):
    return [lax.ppermute(h, "chip", LINKS[ORDERS[s][k]]) for s, h in enumerate(streams)]


def in_hbm(array):
    return pltpu.with_memory_space_constraint(array, pltpu.HBM)


def add_up(block, *refs):
    total = refs[0][block].astype(F32)
    for ref in refs[1:]:
        total = total + ref[block].astype(F32)
    return total


def half_body(kept, came, out, held, sem, offset):
    size = held.shape[1]
    loads = [pltpu.make_async_copy(kept[s], held.at[s], sem.at[s]) for s in range(4)]
    for copy in loads:
        copy.start()
    for s in range(4):
        loads[s].wait()

        def step(i, carry):
            total = held[s, i].astype(F32) + came[s][offset + i].astype(F32)
            out[s][i] = total.astype(BF16)
            return carry

        lax.fori_loop(0, size, step, 0, unroll=4)


def in_vmem(body, name, out_shape, *operands):
    vmem = pl.BlockSpec(memory_space=pltpu.VMEM)
    return pl.pallas_call(
        body,
        out_shape=out_shape,
        in_specs=[vmem] * len(operands),
        out_specs=[vmem] * len(out_shape),
        compiler_params=pltpu.CompilerParams(vmem_limit_bytes=6 * MIB),
        name=name,
    )(*operands)


def combine_half(name, kept, came, offset):
    def body(*refs):
        half_body(refs[:4], refs[4:8], refs[8:12], *refs[12:], offset)

    vmem = pl.BlockSpec(memory_space=pltpu.VMEM)
    return pl.pallas_call(
        body,
        out_shape=[jax.ShapeDtypeStruct(kept[0].shape, BF16)] * 4,
        in_specs=[pl.BlockSpec(memory_space=pl.ANY)] * 4 + [vmem] * 4,
        out_specs=[vmem] * 4,
        scratch_shapes=[pltpu.VMEM((4, *kept[0].shape), BF16), pltpu.SemaphoreType.DMA((4,))],
        compiler_params=pltpu.CompilerParams(vmem_limit_bytes=6 * MIB),
        name=name,
    )(*[in_hbm(k) for k in kept], *came)


def square_body(*refs):
    cut = refs[0].shape[0] // 4
    mine = refs[14]

    def step(i, carry):
        for s in range(4):
            for m in range(3):
                total = add_up((m + 1) * cut + i, refs[s], refs[4 + s])
                refs[8 + s // 2 * 3 + m][s % 2, i] = total.astype(BF16)
            mine[s, i] = add_up(i, refs[s], refs[4 + s])
        return carry

    lax.fori_loop(0, cut, step, 0)


def combine_square(kept, came):
    size, block_len, width = kept[0].shape
    shape = jax.ShapeDtypeStruct((2, size // 4, block_len, width), BF16)
    mine = jax.ShapeDtypeStruct((4, size // 4, block_len, width), F32)
    return in_vmem(square_body, "combine_square", [shape] * 6 + [mine], *kept, *came)


def last_body(mine_in, *refs):
    came, (out_own, out_sib), (mine, held, sem) = refs[:6], refs[6:8], refs[8:]
    loads = [pltpu.make_async_copy(mine_in, mine, sem.at[6])]
    for n in range(6):
        loads.append(pltpu.make_async_copy(came[n], held.at[n], sem.at[n]))
    for copy in loads:
        copy.start()
    for copy in loads:
        copy.wait()

    def step(i, carry):
        for s in range(4):
            pair = s // 2
            total = mine[s, i]
            for n in range(3 * pair, 3 * pair + 3):
                total = total + held[n, s % 2, i].astype(F32)
            (out_sib if s % 2 else out_own)[pair, i] = total.astype(BF16)
        return carry

    lax.fori_loop(0, mine.shape[1], step, 0)


def combine_last(mine, square):
    part = (2, *mine.shape[1:])
    left = pl.BlockSpec(memory_space=pl.ANY)
    vmem = pl.BlockSpec(memory_space=pltpu.VMEM)
    return pl.pallas_call(
        last_body,
        out_shape=[jax.ShapeDtypeStruct(part, BF16)] * 2,
        in_specs=[left] * 7,
        out_specs=[vmem] * 2,
        scratch_shapes=[
            pltpu.VMEM(mine.shape, F32),
            pltpu.VMEM((6, *part), BF16),
            pltpu.SemaphoreType.DMA((7,)),
        ],
        compiler_params=pltpu.CompilerParams(vmem_limit_bytes=6 * MIB),
        name="combine_last",
    )(*[in_hbm(a) for a in (mine, *square)])


def square_join_body(*refs):
    cut = refs[0].shape[1]
    for s in range(4):
        for m in range(4):
            for i in range(cut):
                refs[8 + s][m * cut + i] = refs[2 * m + s // 2][s % 2, i]


def join_square(pairs, came):
    _, cut, block_len, width = pairs[0].shape
    shape = jax.ShapeDtypeStruct((4 * cut, block_len, width), BF16)
    return in_vmem(square_join_body, "join_square", [shape] * 4, *pairs, *came)


def join_body(*refs):
    size = refs[0].shape[0]

    def step(i, carry):
        for s in range(4):
            refs[8 + s][i] = refs[s][i]
            refs[8 + s][size + i] = refs[4 + s][i]
        return carry

    lax.fori_loop(0, size, step, 0, unroll=2)


def join_halves(held, came):
    shape = jax.ShapeDtypeStruct((2 * held[0].shape[0], *held[0].shape[1:]), BF16)
    return in_vmem(join_body, "join_halves", [shape] * 4, *held, *came)


def project_body(core, hid_ref, w_ref, own, other):
    scale = 1.0 / math.sqrt(DH)
    both = jnp.dot(hid_ref[...], w_ref[...], preferred_element_type=F32) * scale
    first, second = both[:, :DH].astype(BF16), both[:, DH:].astype(BF16)

    @pl.when(core[0] == 0)
    def _():
        own[...] = first
        other[...] = second

    @pl.when(core[0] != 0)
    def _():
        own[...] = second
        other[...] = first


def project(core, hidden_rows, query_weight):
    rows, model_width = hidden_rows.shape
    chunk = rows // 8
    out_spec = pl.BlockSpec((chunk, DH), lambda i, p: (i, 0))
    return pl.pallas_call(
        project_body,
        out_shape=[jax.ShapeDtypeStruct((rows, DH), BF16)] * 2,
        grid_spec=pltpu.PrefetchScalarGridSpec(
            num_scalar_prefetch=1,
            grid=(rows // chunk,),
            in_specs=[
                pl.BlockSpec((chunk, model_width), lambda i, p: (i, 0)),
                pl.BlockSpec(query_weight.shape, lambda i, p: (0, 0)),
            ],
            out_specs=[out_spec] * 2,
        ),
        compiler_params=pltpu.CompilerParams(vmem_limit_bytes=12 * MIB),
        name="project",
    )(core, in_hbm(hidden_rows), query_weight)


def weight_sum_body(terms, out):
    total = terms[0].astype(F32)
    for n in range(1, terms.shape[0]):
        total = total + terms[n].astype(F32)
    out[...] = total.T.astype(BF16)


def weight_sum(terms):
    _, head_cols, part = terms.shape
    shape = jax.ShapeDtypeStruct((part, head_cols), BF16)
    return in_vmem(weight_sum_body, "weight_sum", [shape], terms)[0]


def attention_body(
    slots, counts, q_own, q_sib, g_own, g_sib, *refs
):
    kv_in, (ctx_own, gq_own, pair_sib), outs = refs[:8], refs[8:11], refs[11:23]
    kv_all, dk_all, dv_all, in_sem, out_sem = refs[23:]
    scale = 1.0 / math.sqrt(DH)
    block_len = kv_all.shape[1]
    half = dk_all.shape[0] // 4
    loads = []
    for n, ref in enumerate(kv_in):
        part = kv_all.at[pl.ds(n * half, half)]
        loads.append(pltpu.make_async_copy(ref, part, in_sem.at[n]))
    for copy in loads:
        copy.start()
    blank = jnp.zeros(dk_all.shape[1:], BF16)

    def clear(n, carry):
        dk_all[n] = blank
        dv_all[n] = blank
        return carry

    lax.fori_loop(0, dk_all.shape[0], clear, 0, unroll=4)
    for copy in loads:
        copy.wait()
    spans = q_own.shape[0]
    rows = (((1,), (1,)), ((), ()))
    cols = (((0,), (0,)), ((), ()))

    def step(i, carry):
        batch = []
        for part in range(PARTS):
            at = i + part * (spans // PARTS)
            batch += [(q_own, g_own, at, at), (q_sib, g_sib, at, at + spans)]
        q = [qr[n] for qr, _, n, _ in batch]
        g = [gr[n] for _, gr, n, _ in batch]
        refs = [(2 * span, 2 * span + 1) for _, _, _, span in batch]
        k = [jnp.concatenate([kv_all[slots[0, r]] for r in pair], axis=0) for pair in refs]
        v = [jnp.concatenate([kv_all[slots[1, r]] for r in pair], axis=0) for pair in refs]
        s = [lax.dot_general(a, b, rows, preferred_element_type=F32) for a, b in zip(q, k)]
        ga = [lax.dot_general(a, b, rows, preferred_element_type=F32) for a, b in zip(g, v)]
        place = lax.broadcasted_iota(jnp.int32, s[0].shape, 1)
        s = [
            jnp.where(place < counts[span] * block_len, a, -jnp.inf)
            for a, (_, _, _, span) in zip(s, batch)
        ]
        w = [jnp.exp(a - jnp.max(a, axis=1, keepdims=True)) for a in s]
        att = [a / jnp.sum(a, axis=1, keepdims=True) for a in w]
        low = [a.astype(BF16) for a in att]
        gs = [
            (a * (b - jnp.sum(a * b, axis=1, keepdims=True))).astype(BF16)
            for a, b in zip(att, ga)
        ]
        ctx = [jnp.dot(a, b, preferred_element_type=F32).astype(BF16) for a, b in zip(low, v)]
        gq = [(jnp.dot(a, b, preferred_element_type=F32) * scale).astype(BF16) for a, b in zip(gs, k)]
        dk = [lax.dot_general(a, b, cols, preferred_element_type=F32).astype(BF16) for a, b in zip(gs, q)]
        dv = [lax.dot_general(a, b, cols, preferred_element_type=F32).astype(BF16) for a, b in zip(low, g)]
        for n in range(0, len(batch), 2):
            at = batch[n][2]
            ctx_own[at] = ctx[n]
            gq_own[at] = gq[n]
            pair_sib[0, at] = ctx[n + 1]
            pair_sib[1, at] = gq[n + 1]
        for n, pair in enumerate(refs):
            for j, r in enumerate(pair):
                at = slots[2, r]
                part = dk[n][j * block_len : (j + 1) * block_len].astype(F32)
                dk_all[at] = (dk_all[at].astype(F32) + part).astype(BF16)
                at = slots[3, r]
                part = dv[n][j * block_len : (j + 1) * block_len].astype(F32)
                dv_all[at] = (dv_all[at].astype(F32) + part).astype(BF16)
        return carry

    lax.fori_loop(0, spans // PARTS, step, 0)
    stores = []
    for s in range(4):
        whole = dk_all if s < 2 else dv_all
        at = s % 2 * 2 * half
        for ref in outs[3 * s : 3 * s + 3]:
            size = ref.shape[0]
            stores.append(
                pltpu.make_async_copy(whole.at[pl.ds(at, size)], ref, out_sem.at[len(stores)])
            )
            at += size
    for copy in stores:
        copy.start()
    for copy in stores:
        copy.wait()


def attention(slots, counts, q_own, q_sib, g_own, g_sib, gathered):
    spans, span_len, width = q_own.shape
    half, block_len, _ = gathered[0].shape
    small = jax.ShapeDtypeStruct((spans, span_len, width), BF16)
    pair = jax.ShapeDtypeStruct((2, spans, span_len, width), BF16)
    pieces = [half // 2, half // 2, half] * 4
    large = [pltpu.HBM((n, block_len, width), BF16) for n in pieces]
    grads = pltpu.VMEM((4 * half, block_len, width), BF16)
    smem = pl.BlockSpec(memory_space=pltpu.SMEM)
    vmem = pl.BlockSpec(memory_space=pltpu.VMEM)
    hbm = pl.BlockSpec(memory_space=pltpu.HBM)
    left = pl.BlockSpec(memory_space=pl.ANY)
    return pl.pallas_call(
        attention_body,
        out_shape=[small, small, pair] + large,
        in_specs=[smem] * 2 + [vmem] * 4 + [left] * 8,
        out_specs=[vmem] * 3 + [hbm] * 12,
        scratch_shapes=[
            pltpu.VMEM((8 * half, block_len, width), BF16),
            grads,
            grads,
            pltpu.SemaphoreType.DMA((8,)),
            pltpu.SemaphoreType.DMA((12,)),
        ],
        compiler_params=pltpu.CompilerParams(vmem_limit_bytes=20 * MIB),
        name="attention",
    )(slots, counts, q_own, q_sib, g_own, g_sib, *[in_hbm(a) for a in gathered])


def weight_body(core, gq_ref, hid_ref, own, sib, gq_t):
    step = pl.program_id(0)

    @pl.when(step == 0)
    def _():
        gq_t[...] = gq_ref[...].T

    term = jnp.dot(gq_t[...], hid_ref[...], preferred_element_type=F32).astype(BF16)
    chips, _, part = own.shape
    for n in range(chips):
        even = term[:, 2 * n * part : (2 * n + 1) * part]
        odd = term[:, (2 * n + 1) * part : (2 * n + 2) * part]

        @pl.when(core[0] == 0)
        def _():
            own[n] = even
            sib[n] = odd

        @pl.when(core[0] != 0)
        def _():
            own[n] = odd
            sib[n] = even


def weight_terms(core, grad_rows, hidden_rows):
    rows, model_width = hidden_rows.shape
    head_cols = grad_rows.shape[1]
    part = model_width // (2 * CHIPS)
    chips = 2
    wide = 2 * chips * part
    out_spec = pl.BlockSpec((chips, head_cols, part), lambda i, p: (i, 0, 0))
    return pl.pallas_call(
        weight_body,
        out_shape=[jax.ShapeDtypeStruct((CHIPS, head_cols, part), BF16)] * 2,
        grid_spec=pltpu.PrefetchScalarGridSpec(
            num_scalar_prefetch=1,
            grid=(CHIPS // chips,),
            in_specs=[
                pl.BlockSpec(grad_rows.shape, lambda i, p: (0, 0)),
                pl.BlockSpec((rows, wide), lambda i, p: (0, i)),
            ],
            out_specs=[out_spec] * 2,
            scratch_shapes=[pltpu.VMEM(grad_rows.shape[::-1], BF16)],
        ),
        compiler_params=pltpu.CompilerParams(vmem_limit_bytes=12 * MIB),
        name="weight_terms",
    )(core, grad_rows, in_hbm(hidden_rows))


def hidden_body(core, gq_ref, mine, other, out):
    wide = mine.shape[1]
    for n, w_ref in enumerate((mine, other)):
        total = None
        for g in range(gq_ref.shape[0]):
            term = lax.dot_general(
                gq_ref[g], w_ref[g], (((1,), (1,)), ((), ())), preferred_element_type=F32
            )
            term = term.astype(BF16).astype(F32)
            total = term if total is None else total + term
        at = pl.multiple_of((core[0] if n == 0 else 1 - core[0]) * wide, wide)
        out[:, pl.ds(at, wide)] = total.astype(BF16)


def hidden_grads(core, every_grad, mine, other):
    groups, rows, head_cols = every_grad.shape
    wide = 2 * mine.shape[1]
    chunk = rows // 4
    return pl.pallas_call(
        hidden_body,
        out_shape=jax.ShapeDtypeStruct((rows, wide), BF16),
        grid_spec=pltpu.PrefetchScalarGridSpec(
            num_scalar_prefetch=1,
            grid=(rows // chunk,),
            in_specs=[
                pl.BlockSpec((groups, chunk, head_cols), lambda i, p: (0, i, 0)),
                pl.BlockSpec(mine.shape, lambda i, p: (0, 0, 0)),
                pl.BlockSpec(mine.shape, lambda i, p: (0, 0, 0)),
            ],
            out_specs=pl.BlockSpec((chunk, wide), lambda i, p: (i, 0)),
        ),
        compiler_params=pltpu.CompilerParams(vmem_limit_bytes=16 * MIB),
        name="hidden_grads",
    )(core, in_hbm(every_grad), mine, other)


def per_device(hidden, query_weight, keys, values, neighbour_ids, neighbour_counts, d_context):
    spans, span_len, model_width = hidden.shape
    blocks, block_len, head_cols = keys.shape
    groups = lax.axis_size("grp")
    chip = lax.axis_index("chip")
    core = lax.axis_index("core")
    core_at = core.reshape(1)
    rows = spans * span_len
    refs = neighbour_ids.size

    def both(array):
        first, second = array[..., :DH], array[..., DH:]
        return jnp.where(core == 0, first, second), jnp.where(core == 0, second, first)

    def joined(own, other):
        return jnp.where(
            core == 0,
            jnp.concatenate([own, other], axis=-1),
            jnp.concatenate([other, own], axis=-1),
        )

    with jax.named_scope("gather"):
        own, other = both(jnp.stack([keys, values]))
        came = swap(other)
        pairs = lax.optimization_barrier(
            [jnp.stack([own[0], came[0]]), jnp.stack([own[1], came[1]])]
        )

        def across(pieces, k):
            return [lax.ppermute(p, "chip", LINKS[ORDERS[s][k]]) for s, p in enumerate(pieces)]

        came = [
            lax.ppermute(pairs[pair], "chip", square_pairs(pair, m))
            for m in (1, 2, 3)
            for pair in range(2)
        ]
        held = join_square(pairs, came)
        held = join_halves(held, across(held, 2))
        last = across(held, 3)
    with jax.named_scope("queries"):
        hidden_rows = hidden.reshape(rows, model_width)
        query_own, query_other = project(core_at, hidden_rows, query_weight)
        query_own, query_other, leaving = lax.optimization_barrier(
            (query_own, query_other, query_weight)
        )
        last, query_own, query_other = lax.optimization_barrier((last, query_own, query_other))
        gathered = [part for parts in zip(held, last) for part in parts]
        query_own = query_own.reshape(spans, span_len, DH)
        query_sib = swap(query_other.reshape(spans, span_len, DH))
    with jax.named_scope("weight_rows"):
        wide = model_width // groups
        asked = leaving.reshape(groups, 2, wide // 2, head_cols)
        asked = jnp.where(core == 0, asked[:, 0], asked[:, 1])
        weight_own = lax.all_to_all(asked, "grp", split_axis=0, concat_axis=0, tiled=True)
    with jax.named_scope("more"):
        grad_own, grad_other = both(d_context)
        grad_sib = swap(grad_other)
    with jax.named_scope("slots"):
        table = jnp.concatenate([neighbour_ids.reshape(-1), neighbour_counts])
        table_sib = swap(table)
        ids = jnp.concatenate([table[:refs], table_sib[:refs]])
        counts = jnp.concatenate([table[refs:], table_sib[refs:]])
        owner, local = ids // blocks, ids % blocks
        far = jnp.where(owner % 2 == core, 0, 1)
        host = owner // 2

        def slot(orders, first):
            near_place = cube_place(chip, host, orders[0])
            far_place = CHIPS + cube_place(chip, host, orders[1])
            return (first + jnp.where(far == 0, near_place, far_place)) * blocks + local

        slots = jnp.stack(
            [
                slot(ORDERS[:2], 0),
                slot(ORDERS[2:], 2 * CHIPS),
                slot(ORDERS[:2], 0),
                slot(ORDERS[2:], 0),
            ]
        )
    with jax.named_scope("attend"):
        out = attention(slots, counts, query_own, query_sib, grad_own, grad_sib, gathered)
        ctx_own, gq_own, pair_sib = out[:3]
        low, mid, high = out[3::3], out[4::3], out[5::3]
    with jax.named_scope("grad_queries"):
        pair = swap(pair_sib)
        grad_rows = joined(gq_own, pair[1]).reshape(rows, head_cols)
        grad_rows, high, weight_own = lax.optimization_barrier((grad_rows, high, weight_own))
        weight_other = swap(weight_own)
        every_grad = lax.all_gather(grad_rows, "grp", axis=0, tiled=False)
    with jax.named_scope("return"):
        first = send(high, 3)
        terms, terms_sib = weight_terms(core_at, grad_rows, hidden_rows)
        context = joined(ctx_own, pair[0])
        first, terms, terms_sib, context = lax.optimization_barrier((first, terms, terms_sib, context))
        halved = combine_half("combine_high", mid, first, mid[0].shape[0])
        halved, terms, terms_sib = lax.optimization_barrier((halved, terms, terms_sib))
        second = send(halved, 2)
        terms = (terms.astype(F32) + swap(terms_sib).astype(F32)).astype(BF16)
        stays = combine_half("combine_low", low, first, 0)
        second, stays, terms = lax.optimization_barrier((second, stays, terms))
        *square, mine = combine_square(stays, second)
        square = [
            lax.ppermute(square[3 * pair + m], "chip", square_pairs(pair, m + 1))
            for pair in range(2)
            for m in range(3)
        ]
        square, mine, terms = lax.optimization_barrier((square, mine, terms))
        terms = lax.all_to_all(terms, "chip", split_axis=0, concat_axis=0, tiled=True)
        d_hidden = hidden_grads(core_at, every_grad, weight_own, weight_other)
        sums, sums_sib = combine_last(mine, square)
        other = swap(sums_sib)
        other, d_hidden = lax.optimization_barrier((other, d_hidden))
        d_hidden, terms = lax.optimization_barrier((d_hidden, terms))
        d_keys = joined(sums[0], other[0])
        d_values = joined(sums[1], other[1])
        d_weight = weight_sum(terms)
        d_hidden = d_hidden.reshape(spans, span_len, wide)
    return context, d_hidden, d_keys, d_values, d_weight


def solution(mesh):
    fine = Mesh(mesh.devices.reshape(mesh.devices.shape[0], CHIPS, 2), ("grp", "chip", "core"))
    placed = (
        P(NB, None, None),
        P(None, "grp"),
        P(NB, None, "grp"),
        P(NB, None, "grp"),
        P(NB, None),
        P(NB),
        P(NB, None, "grp"),
    )
    return jax.shard_map(
        per_device,
        mesh=fine,
        in_specs=placed,
        out_specs=(
            P(NB, None, "grp"),
            P(NB, None, "grp"),
            P(NB, None, "grp"),
            P(NB, None, "grp"),
            P(NB, "grp"),
        ),
        check_vma=False,
    )
```
